1024 devices in a mesh: gx: 16 (over x, core), gy: 64 (over y, z).
Axes of the slice: x: 8, y: 8, z: 8, core: 2. Of those that a mesh axis runs over, the one named last changes fastest.
Arguments:
- model_state: float32 [64, 2048, 528], P('gx', 'gy'), may hold values from -6 to 6
- hyper_coef: float32 [528], replicated, may hold values from 0.0001 to 0.001
- point_mass: float32 [64, 2048], P('gx', 'gy'), may hold values from 0.5 to 2
- inverse_mass: float32 [64, 2048], P('gx', 'gy'), may hold values from 0.2 to 0.8
- span_slot: int32 [64, 2048], P('gx', 'gy'), may hold values from 0 to 2047, as said below
- vert_diff: float32 [64, 48, 2048], P('gy', None, 'gx'), may hold values from 0.05 to 20
- fall_rate: float32 [64, 48, 2048], P('gy', None, 'gx'), may hold values from 0.1 to 10
- cloud_frac: float32 [64, 48, 2048], P('gy', None, 'gx'), may hold values from 0 to 1
Outputs:
- new_state: float32 [64, 2048, 528], P('gx', 'gy')
The draws below stay inside these ranges and needn't reach their ends.
Inputs may be any that keep to these rules, and one draw needn't show every extreme that they name: `span_slot`: within the columns that share a block of 32 along the second dimension, the values form a permutation; each device's 128 columns hold exactly 8 values in each range from p * 128 to (p + 1) * 128 - 1.
All inputs are finite; a program needn't handle non-finite values.
Results may differ from the reference program's by a relative error of at most 0.0003.
Values sent between devices are 32-bit elements; how exact they have to be, the bound alone decides.
A program may use at most 32 MiB of HBM per device.

```python
import math
import jax
import jax.numpy as jnp
import numpy as np
from jax import lax

NLEV = 48
FLD = 528
PTS_X = 4
PTS_Y = 32
COLS = 128
PER = 8
NXP = 64
NYP = 2048
PHYS = 2048
BLOCKS_Y = 64
N_GX = 16
N_GY = 64


def draw_span_slot(key, part):
    key_first, key_second = jax.random.split(jax.random.fold_in(key, 7))
    keys_first = jax.random.split(key_first, N_GY * N_GX)
    keys_second = jax.random.split(key_second, N_GY * N_GX)
    first_perm = jax.vmap(lambda one_key: jax.random.permutation(one_key, COLS))(keys_first).reshape(N_GY, N_GX, COLS)
    second_perm = jax.vmap(lambda one_key: jax.random.permutation(one_key, COLS))(keys_second).reshape(N_GY, N_GX, COLS)
    target = first_perm // PER
    incoming = jnp.arange(N_GX)[None, :, None] * PER + first_perm % PER
    group_index = jnp.arange(N_GY)[:, None, None]
    within = second_perm[group_index, target, incoming]
    position_labels = (target * COLS + within).astype(jnp.int32)
    grid = position_labels.reshape(N_GY, N_GX, PTS_X, PTS_Y)
    return jnp.transpose(grid, (1, 2, 0, 3)).reshape(NXP, NYP)


def block_levels(key, extent, pieces, smallest, largest):
    loudness = 1.0
    for dim, blocks in pieces:
        heights = jax.random.uniform(jax.random.fold_in(jax.random.fold_in(key, 6), dim), (blocks,), jnp.float32, smallest / len(pieces), largest / len(pieces))
        loudness = loudness * jnp.repeat(jnp.exp(heights), extent[dim] // blocks).reshape((-1,) + (1,) * (len(extent) - 1 - dim))
    return loudness


def bell_draw(own_key, extent, width, most, shards=(), dtype=jnp.bfloat16):
    result = width * jax.random.normal(own_key, extent, jnp.float32)
    if shards:
        result = result * block_levels(own_key, extent, shards, -0.22, 0.18)
    return jnp.clip(result, -most, most).astype(dtype)


def setup_inputs(seed: int = 0) -> dict:
    streams_of = jax.random.split(jax.random.key(seed), 9)
    model_state = bell_draw(streams_of[0], (NXP, NYP, FLD), 1.0, 6.0, ((0, 16), (1, 64)), jnp.float32)
    hyper_coef = jnp.clip(jnp.exp(jax.random.uniform(streams_of[1], (FLD,), jnp.float32, math.log(0.0001), math.log(0.001))), 0.0001, 0.001)
    point_mass = jnp.clip(jnp.exp(math.log(2.0) - 1.3862944 * jax.random.uniform(streams_of[2], (NXP, NYP), jnp.float32) ** block_levels(streams_of[2], (NXP, NYP), ((0, 16), (1, 64)), -0.2, 0.2)), 0.5, 2.0)
    inverse_mass = jnp.clip(jnp.exp(math.log(0.8) - 1.3862944 * jax.random.uniform(streams_of[3], (NXP, NYP), jnp.float32) ** block_levels(streams_of[3], (NXP, NYP), ((0, 16), (1, 64)), -0.2, 0.2)), 0.2, 0.8)
    span_slot = draw_span_slot(jax.random.fold_in(streams_of[8], 71), 0)
    vert_diff = jnp.clip(jnp.exp(math.log(20.0) - 5.9914645 * jax.random.uniform(streams_of[5], (BLOCKS_Y, NLEV, PHYS), jnp.float32) ** block_levels(streams_of[5], (BLOCKS_Y, NLEV, PHYS), ((0, 64), (2, 16)), -0.2, 0.2)), 0.05, 20.0)
    fall_rate = jnp.clip(jnp.exp(math.log(10.0) - 4.6051702 * jax.random.uniform(streams_of[6], (BLOCKS_Y, NLEV, PHYS), jnp.float32) ** block_levels(streams_of[6], (BLOCKS_Y, NLEV, PHYS), ((0, 64), (2, 16)), -0.2, 0.2)), 0.1, 10.0)
    cloud_frac = jnp.clip(1.0 * jax.random.uniform(streams_of[7], (BLOCKS_Y, NLEV, PHYS), jnp.float32) ** block_levels(streams_of[7], (BLOCKS_Y, NLEV, PHYS), ((0, 64), (2, 16)), -0.2, 0.2), 0.0, 1.0)
    return dict(model_state=model_state, hyper_coef=hyper_coef, point_mass=point_mass, inverse_mass=inverse_mass, span_slot=span_slot, vert_diff=vert_diff, fall_rate=fall_rate, cloud_frac=cloud_frac)


def second_table():
    nodes = np.array([-1.0, -1.0 / np.sqrt(5.0), 1.0 / np.sqrt(5.0), 1.0])
    deriv = np.zeros((4, 4))
    for row_index in range(4):
        for col_index in range(4):
            if row_index == col_index:
                deriv[row_index, col_index] = sum((1.0 / (nodes[row_index] - nodes[other]) for other in range(4) if other != row_index))
            else:
                upper_part = np.prod([nodes[row_index] - nodes[other] for other in range(4) if other != row_index])
                lower_part = np.prod([nodes[col_index] - nodes[other] for other in range(4) if other != col_index])
                deriv[row_index, col_index] = upper_part / (lower_part * (nodes[row_index] - nodes[col_index]))
    return deriv @ deriv

def harmonic_operator(field):
    second_deriv = jnp.asarray(second_table(), jnp.float32)
    size_x, size_y, row_width = field.shape
    along_x = jnp.einsum('ab,ebyf->eayf', second_deriv, field.reshape(size_x // 4, 4, size_y, row_width), precision=lax.Precision.HIGHEST).reshape(size_x, size_y, row_width)
    along_y = jnp.einsum('ab,xebf->xeaf', second_deriv, field.reshape(size_x, size_y // 4, 4, row_width), precision=lax.Precision.HIGHEST).reshape(size_x, size_y, row_width)
    return along_x + along_y

def assemble(values, point_mass, inverse_mass):
    weighted = point_mass[:, :, None] * values
    size_x, size_y = point_mass.shape
    first_x = (jnp.arange(size_x) % 4 == 0)[:, None, None]
    last_x = (jnp.arange(size_x) % 4 == 3)[:, None, None]
    first_y = (jnp.arange(size_y) % 4 == 0)[None, :, None]
    last_y = (jnp.arange(size_y) % 4 == 3)[None, :, None]
    total = weighted + jnp.where(first_x, jnp.roll(weighted, 1, 0), 0.0) + jnp.where(last_x, jnp.roll(weighted, -1, 0), 0.0)
    total = total + jnp.where(first_y, jnp.roll(weighted, 1, 1), 0.0) + jnp.where(last_y, jnp.roll(weighted, -1, 1), 0.0)
    total = total + jnp.where(first_x & first_y, jnp.roll(weighted, (1, 1), (0, 1)), 0.0)
    total = total + jnp.where(first_x & last_y, jnp.roll(weighted, (1, -1), (0, 1)), 0.0)
    total = total + jnp.where(last_x & first_y, jnp.roll(weighted, (-1, 1), (0, 1)), 0.0)
    total = total + jnp.where(last_x & last_y, jnp.roll(weighted, (-1, -1), (0, 1)), 0.0)
    return inverse_mass[:, :, None] * total

def physics(fields, diff_coef, fall_coef, overcast_fraction_weight):
    zero_row = jnp.zeros_like(diff_coef[:1])
    above = jnp.concatenate([zero_row, diff_coef[1:]], 0)
    below = jnp.concatenate([diff_coef[1:], zero_row], 0)
    surface = jnp.concatenate([jnp.zeros_like(diff_coef[1:]), diff_coef[:1]], 0)
    centre = 1.0 + above + below + surface

    def forward(state_carry, inputs):
        prev_gain, previous_value = state_carry
        sub_k, centre_k, sup_k, rhs_k = inputs
        divisor = centre_k - sub_k * prev_gain
        gain = sup_k / divisor
        value = (rhs_k + sub_k[None, :] * previous_value) / divisor[None, :]
        return ((gain, value), (gain, value))
    start = (jnp.zeros_like(diff_coef[0]), jnp.zeros_like(fields[0]))
    _, (gains, values) = lax.scan(forward, start, (above, centre, below, fields))

    def backward(next_solved, inputs):
        gain, value = inputs
        solved_line_entries = value + gain[None, :] * next_solved
        return (solved_line_entries, solved_line_entries)
    _, solved_line_entries = lax.scan(backward, jnp.zeros_like(fields[0]), (gains, values), reverse=True)
    thermal_state_kelvin = solved_line_entries[:, 0]
    humidity_mixing_ratio = solved_line_entries[:, 1]
    droplet_mixing_ratio = solved_line_entries[:, 2]
    condensed_mass_content = overcast_fraction_weight * 0.5 * jnp.maximum(humidity_mixing_ratio - 0.3 * thermal_state_kelvin, 0.0)
    humidity_mixing_ratio = humidity_mixing_ratio - condensed_mass_content
    droplet_mixing_ratio = droplet_mixing_ratio + condensed_mass_content
    thermal_state_kelvin = thermal_state_kelvin + 2.0 * condensed_mass_content

    def settle(inflow, inputs):
        liquid_k, fall_k = inputs
        settled = (liquid_k + inflow) / (1.0 + fall_k)
        return (fall_k * settled, settled)
    _, droplet_mixing_ratio = lax.scan(settle, jnp.zeros_like(droplet_mixing_ratio[0]), (droplet_mixing_ratio, fall_coef))
    return jnp.concatenate([thermal_state_kelvin[:, None], humidity_mixing_ratio[:, None], droplet_mixing_ratio[:, None], solved_line_entries[:, 3:]], 1)

def reference(model_state, hyper_coef, point_mass, inverse_mass, span_slot, vert_diff, fall_rate, cloud_frac):
    lap_once = assemble(harmonic_operator(model_state), point_mass, inverse_mass)
    lap_twice = assemble(harmonic_operator(lap_once), point_mass, inverse_mass)
    dynamic = model_state - hyper_coef[None, None, :] * lap_twice
    size_x, size_y, row_width = dynamic.shape
    levels = vert_diff.shape[1]
    variables = row_width // levels
    block_cols = size_x * PTS_Y
    dyn_blocks = dynamic.reshape(size_x, BLOCKS_Y, PTS_Y, row_width).transpose(1, 0, 2, 3)
    slot_blocks = span_slot.reshape(size_x, BLOCKS_Y, PTS_Y).transpose(1, 0, 2)

    def one_block(items):
        block_state, block_slot, diff_block, fall_block, cloud_block = items
        fields = block_state.reshape(block_cols, variables, levels).transpose(2, 1, 0)
        index = block_slot.reshape(block_cols).astype(jnp.int32)
        updated = physics(fields, jnp.take(diff_block, index, axis=1), jnp.take(fall_block, index, axis=1), jnp.take(cloud_block, index, axis=1))
        tendency = updated - fields
        return (fields + tendency).transpose(2, 1, 0).reshape(size_x, PTS_Y, row_width)
    blocks = lax.map(one_block, (dyn_blocks, slot_blocks, vert_diff, fall_rate, cloud_frac))
    return blocks.transpose(1, 0, 2, 3).reshape(size_x, size_y, row_width)
```

```python
import functools

import jax
import jax.numpy as jnp
import numpy as np
from jax import lax
from jax.experimental import pallas as pl
from jax.experimental.pallas import tpu as pltpu
from jax.sharding import PartitionSpec as P

MESH = pl.DeviceIdType.MESH
F32 = jnp.float32
BF16 = jnp.bfloat16
NX, NY, COLS, LEV, VARS = 4, 32, 128, 48, 11
FLD = LEV * VARS
COEF = 3 * LEV


def second_table():
    nodes = np.array([-1.0, -1.0 / np.sqrt(5.0), 1.0 / np.sqrt(5.0), 1.0])
    deriv = np.zeros((4, 4))
    for i in range(4):
        for j in range(4):
            if i == j:
                deriv[i, j] = sum(1.0 / (nodes[i] - nodes[o]) for o in range(4) if o != i)
            else:
                upper = np.prod([nodes[i] - nodes[o] for o in range(4) if o != i])
                lower = np.prod([nodes[j] - nodes[o] for o in range(4) if o != j])
                deriv[i, j] = upper / (lower * (nodes[i] - nodes[j]))
    return (deriv @ deriv).astype(np.float32)


def tables():
    second = second_table()
    x, y = np.divmod(np.arange(COLS), NY)
    same_x = x[:, None] == x[None, :]
    same_y = y[:, None] == y[None, :]
    same_e = (y[:, None] // 4) == (y[None, :] // 4)
    lap = np.where(same_y, second[x[:, None], x[None, :]], 0.0)
    lap = lap + np.where(same_x & same_e, second[y[:, None] % 4, y[None, :] % 4], 0.0)
    twin = np.where(y % 4 == 0, y - 1, np.where(y % 4 == 3, y + 1, -5))
    pick = np.eye(COLS) + np.where(same_x & (y[None, :] == twin[:, None]), 1.0, 0.0)
    edge = np.zeros((8, COLS))
    for i in range(4):
        edge[i, i * NY] = 1.0
        edge[4 + i, i * NY + NY - 1] = 1.0
    return lap.astype(np.float32), np.concatenate([pick, edge], 0).astype(np.float32)


def split(value):
    high = value.astype(BF16)
    return high, (value - high.astype(F32)).astype(BF16)


def dot(a, b):
    return jnp.dot(a, b, preferred_element_type=F32)


def exact(a, b, dims):
    return lax.dot_general(
        a, b, (dims, ((), ())), precision=lax.Precision.HIGHEST, preferred_element_type=F32
    )


def iota(shape, dim):
    return lax.broadcasted_iota(jnp.int32, shape, dim)


def body(
    n_gx, n_gy,
    state, hyper, pmass, imass, slots, vdiff, frate, cfrac, lap, pick,
    out,
    v, tsum, edges, xin, yin, cin, small, sl, coef, sent, got, lap_s, pick_s, hyp,
    dyn, tr, fac, wk, res,
    in_sem, out_sem, hs_sem, hr_sem, ss_sem, sr_sem, cs_sem, cr_sem,
):
    per = COLS // n_gx
    me = lax.axis_index("gx")
    my = lax.axis_index("gy")
    left, right = lax.rem(me + n_gx - 1, n_gx), lax.rem(me + 1, n_gx)
    down, up = lax.rem(my + n_gy - 1, n_gy), lax.rem(my + 1, n_gy)
    peers = [lax.rem(me + i, n_gx) for i in range(1, n_gx)]
    around = [(left, my), (right, my), (me, down), (me, up),
              (left, down), (left, up), (right, down), (right, up)]

    barrier = pltpu.get_barrier_semaphore()
    for target in around[2:] + [(q, my) for q in peers]:
        pl.semaphore_signal(barrier, inc=1, device_id=target, device_id_type=MESH)

    loads = [
        pltpu.make_async_copy(slots, sl.at[me], in_sem.at[0]),
        pltpu.make_async_copy(pmass, small.at[0], in_sem.at[1]),
        pltpu.make_async_copy(imass, small.at[1], in_sem.at[2]),
        pltpu.make_async_copy(lap, lap_s, in_sem.at[3]),
        pltpu.make_async_copy(pick, pick_s, in_sem.at[4]),
        pltpu.make_async_copy(vdiff.at[0], coef.at[pl.ds(0, LEV)], in_sem.at[5]),
        pltpu.make_async_copy(frate.at[0], coef.at[pl.ds(LEV, LEV)], in_sem.at[6]),
        pltpu.make_async_copy(cfrac.at[0], coef.at[pl.ds(2 * LEV, LEV)], in_sem.at[7]),
        pltpu.make_async_copy(hyper, hyp, in_sem.at[8]),
    ] + [
        pltpu.make_async_copy(state.at[x], v.at[pl.ds(NY * x, NY)], in_sem.at[9 + x])
        for x in range(NX)
    ]
    for load in loads:
        load.start()

    rows, lanes = iota((COLS, COLS), 0), iota((COLS, COLS), 1)
    eye = rows == lanes
    tri = jnp.where(rows < lanes, 1.0, 0.0).astype(BF16)

    def as_row(block):
        return jnp.concatenate([block[x : x + 1, :] for x in range(NX)], axis=1)

    for i in (1, 2, 3, 4):
        loads[i].wait()
    mass_row = as_row(small[0])
    inv_row = as_row(small[1])
    inv_col = jnp.sum(jnp.where(eye, inv_row, 0.0), axis=1, keepdims=True)
    op_high, op_low = split(exact(pick_s[...] * mass_row, lap_s[...], ((1,), (0,))))

    def weigh(r, field):
        high, low = split(field)
        total = dot(op_high, high) + (dot(op_high, low) + dot(op_low, high))
        tsum[r] = total[:COLS]
        for i in range(8):
            edges[r, i] = total[COLS + i : COLS + i + 1]

    def halo(r):
        plan = [
            (tsum.at[r, pl.ds(0, NY)], xin.at[r, 1]),
            (tsum.at[r, pl.ds(COLS - NY, NY)], xin.at[r, 0]),
            (edges.at[r, pl.ds(0, 4)], yin.at[r, 1]),
            (edges.at[r, pl.ds(4, 4)], yin.at[r, 0]),
            (edges.at[r, 0], cin.at[r, 3]),
            (edges.at[r, 4], cin.at[r, 2]),
            (edges.at[r, 3], cin.at[r, 1]),
            (edges.at[r, 7], cin.at[r, 0]),
        ]
        return [
            pltpu.make_async_remote_copy(
                src_ref=src, dst_ref=dst, send_sem=hs_sem.at[r, i], recv_sem=hr_sem.at[r, i],
                device_id=around[i], device_id_type=MESH,
            )
            for i, (src, dst) in enumerate(plan)
        ]

    def assemble(r):
        acc = tsum.at[r]
        acc[pl.ds(0, NY), :] = acc[pl.ds(0, NY), :] + xin[r, 0]
        acc[pl.ds(COLS - NY, NY), :] = acc[pl.ds(COLS - NY, NY), :] + xin[r, 1]
        corner = {0: (0, 1), 3: (2, 3)}
        for x in range(NX):
            low, high = yin[r, 0, x], yin[r, 1, x]
            if x in corner:
                low = low + cin[r, corner[x][0]]
                high = high + cin[r, corner[x][1]]
            acc[pl.ds(NY * x, 1), :] = acc[pl.ds(NY * x, 1), :] + low
            acc[pl.ds(NY * x + NY - 1, 1), :] = acc[pl.ds(NY * x + NY - 1, 1), :] + high
        return inv_col * acc[...]

    for x in range(NX):
        loads[9 + x].wait()
    weigh(0, v[...])
    loads[0].wait()

    pl.semaphore_wait(barrier, n_gx - 1 + 6)

    slot_sends = [
        pltpu.make_async_remote_copy(
            src_ref=sl.at[me], dst_ref=sl.at[me], send_sem=ss_sem.at[i], recv_sem=sr_sem.at[me],
            device_id=(q, my), device_id_type=MESH,
        )
        for i, q in enumerate(peers)
    ]
    for copy in slot_sends:
        copy.start()
    first = halo(0)
    for copy in first:
        copy.start()

    own = as_row(sl[me])
    span = own // COLS
    member = jnp.where(span == iota((n_gx, COLS), 0), 1.0, 0.0)
    before = dot(member.astype(BF16), tri)
    rank = jnp.sum(member * before, axis=0, keepdims=True)
    place = span * per + rank.astype(jnp.int32)
    order = jnp.where(rows == place, 1.0, 0.0)

    for i in (5, 6, 7):
        loads[i].wait()
    for q in peers:
        pltpu.make_async_remote_copy(
            src_ref=sl.at[q], dst_ref=sl.at[q], send_sem=ss_sem.at[0], recv_sem=sr_sem.at[q],
            device_id=(q, my), device_id_type=MESH,
        ).wait_recv()
    every = jnp.concatenate([sl[:, x, :] for x in range(NX)], axis=1)
    mine = (every // COLS) == me
    member = jnp.where(mine, 1.0, 0.0)
    before = dot(member.astype(BF16), tri)
    ranked = jnp.where(mine, before, -1.0).astype(BF16)
    within = (every % COLS).astype(F32).astype(BF16)
    spread = jnp.where(
        iota((COLS, n_gx), 0) // per == iota((COLS, n_gx), 1), 1.0, 0.0
    ).astype(BF16)
    hit = dot(spread, ranked) == (rows % per).astype(F32)
    chosen = jnp.sum(jnp.where(hit, dot(spread, within), 0.0), axis=1, keepdims=True)
    onehot = jnp.where(chosen == lanes.astype(F32), 1.0, 0.0)
    picked = exact(onehot, coef[...], ((1,), (1,)))
    sent[...] = picked.reshape(n_gx, per, COEF)
    coef_sends = [
        pltpu.make_async_remote_copy(
            src_ref=sent.at[q], dst_ref=got.at[me], send_sem=cs_sem.at[i], recv_sem=cr_sem.at[me],
            device_id=(q, my), device_id_type=MESH,
        )
        for i, q in enumerate(peers)
    ]
    for copy in coef_sends:
        copy.start()
    got[me] = sent[me]

    for copy in first:
        copy.wait_recv()
    first[0].wait_send()
    first[1].wait_send()
    weigh(1, assemble(0))
    second = halo(1)
    for copy in second:
        copy.start()

    for q in peers:
        pltpu.make_async_remote_copy(
            src_ref=sent.at[q], dst_ref=got.at[q], send_sem=cs_sem.at[0], recv_sem=cr_sem.at[q],
            device_id=(q, my), device_id_type=MESH,
        ).wait_recv()
    mat = exact(got[...].reshape(COLS, COEF), order, ((0,), (0,)))
    diff, fall, cloud = mat[:LEV], mat[LEV : 2 * LEV], mat[2 * LEV :]
    level = iota((LEV, COLS), 0)
    above = jnp.where(level == 0, 0.0, diff)
    below = jnp.where(level == LEV - 1, 0.0, pltpu.roll(diff, LEV - 1, 0))
    surface = jnp.where(level == LEV - 1, diff[0:1], 0.0)
    centre = 1.0 + above + below + surface
    fac[0] = above
    fac[1] = below
    fac[2] = centre
    gain = jnp.zeros((1, COLS), F32)
    for k in range(LEV):
        a, b, c = (fac[j, pl.ds(k, 1), :] for j in range(3))
        scale = 1.0 / (c - a * gain)
        gain = b * scale
        fac[0, pl.ds(k, 1), :] = a * scale
        fac[1, pl.ds(k, 1), :] = gain
        fac[2, pl.ds(k, 1), :] = scale
    settle = 1.0 / (1.0 + fall)
    inflow = jnp.where(level == 0, 0.0, pltpu.roll(fall, 1, 0)) * settle
    fac[3] = settle
    fac[4] = inflow
    fac[5] = cloud * 0.5

    loads[8].wait()
    for copy in second:
        copy.wait_recv()
    second[0].wait_send()
    second[1].wait_send()
    dyn[:, pl.ds(0, FLD)] = v[...] - hyp[...] * assemble(1)
    for j in range(5):
        tr[pl.ds(COLS * j, COLS), :] = dyn[:, pl.ds(COLS * j, COLS)].T

    def strided(k):
        return pl.ds(k, VARS, stride=LEV)

    value = jnp.zeros((VARS, COLS), F32)
    for k in range(LEV):
        value = tr[strided(k), :] * fac[2, pl.ds(k, 1), :] + fac[0, pl.ds(k, 1), :] * value
        wk[k] = value
    value = jnp.zeros((VARS, COLS), F32)
    for k in reversed(range(LEV)):
        value = wk[k] + fac[1, pl.ds(k, 1), :] * value
        tr[strided(k), :] = value

    heat, vapour, liquid = (tr[pl.ds(LEV * j, LEV), :] for j in range(3))
    moved = fac[5] * jnp.maximum(vapour - 0.3 * heat, 0.0)
    tr[pl.ds(0, LEV), :] = heat + 2.0 * moved
    tr[pl.ds(LEV, LEV), :] = vapour - moved
    fac[3] = (liquid + moved) * fac[3]
    drop = jnp.zeros((1, COLS), F32)
    for k in range(LEV):
        drop = fac[3, pl.ds(k, 1), :] + fac[4, pl.ds(k, 1), :] * drop
        tr[pl.ds(2 * LEV + k, 1), :] = drop

    for j in range(5):
        width = min(COLS, FLD - COLS * j)
        res[:, pl.ds(COLS * j, width)] = tr[pl.ds(COLS * j, COLS), :].T[:, :width]
    stores = [
        pltpu.make_async_copy(res.at[pl.ds(NY * x, NY)], out.at[x], out_sem.at[x])
        for x in range(NX)
    ]
    for store in stores:
        store.start()
    for copy in slot_sends + coef_sends + first[2:] + second[2:]:
        copy.wait_send()
    for store in stores:
        store.wait()


def solution(mesh):
    n_gx, n_gy = mesh.shape["gx"], mesh.shape["gy"]
    per = COLS // n_gx
    lap, pick = tables()
    anywhere = pl.BlockSpec(memory_space=pl.ANY)
    dma = pltpu.SemaphoreType.DMA

    def local(state, hyper, pmass, imass, slots, vdiff, frate, cfrac):
        return pl.pallas_call(
            functools.partial(body, n_gx, n_gy),
            out_shape=jax.ShapeDtypeStruct((NX, NY, FLD), F32),
            in_specs=[anywhere] * 10,
            out_specs=anywhere,
            scratch_shapes=[
                pltpu.VMEM((COLS, FLD), F32),
                pltpu.VMEM((2, COLS, FLD), F32),
                pltpu.VMEM((2, 8, 1, FLD), F32),
                pltpu.VMEM((2, 2, NY, FLD), F32),
                pltpu.VMEM((2, 2, 4, 1, FLD), F32),
                pltpu.VMEM((2, 4, 1, FLD), F32),
                pltpu.VMEM((2, NX, NY), F32),
                pltpu.VMEM((n_gx, NX, NY), jnp.int32),
                pltpu.VMEM((COEF, COLS), F32),
                pltpu.VMEM((n_gx, per, COEF), F32),
                pltpu.VMEM((n_gx, per, COEF), F32),
                pltpu.VMEM((COLS, COLS), F32),
                pltpu.VMEM((COLS + 8, COLS), F32),
                pltpu.VMEM((1, FLD), F32),
                pltpu.VMEM((COLS, 5 * COLS), F32),
                pltpu.VMEM((5 * COLS, COLS), F32),
                pltpu.VMEM((6, LEV, COLS), F32),
                pltpu.VMEM((LEV, VARS, COLS), F32),
                pltpu.VMEM((COLS, FLD), F32),
                dma((13,)),
                dma((NX,)),
                dma((2, 8)),
                dma((2, 8)),
                dma((n_gx,)),
                dma((n_gx,)),
                dma((n_gx,)),
                dma((n_gx,)),
            ],
            compiler_params=pltpu.CompilerParams(collective_id=0, has_side_effects=True),
        )(state, hyper.reshape(1, FLD), pmass, imass, slots, vdiff, frate, cfrac,
          jnp.asarray(lap), jnp.asarray(pick))

    placed = (
        P("gx", "gy", None), P(), P("gx", "gy"), P("gx", "gy"), P("gx", "gy"),
        P("gy", None, "gx"), P("gy", None, "gx"), P("gy", None, "gx"),
    )
    return jax.shard_map(
        local, mesh=mesh, in_specs=placed, out_specs=P("gx", "gy", None), check_vma=False
    )
```

```python
import functools

import jax
import jax.numpy as jnp
import numpy as np
from jax import lax
from jax.experimental import pallas as pl
from jax.experimental.pallas import tpu as pltpu
from jax.sharding import PartitionSpec as P

MESH = pl.DeviceIdType.MESH
F32 = jnp.float32
BF16 = jnp.bfloat16
NX, NY, COLS, LEV, VARS = 4, 32, 128, 48, 11
FLD = LEV * VARS


def second_table():
    nodes = np.array([-1.0, -1.0 / np.sqrt(5.0), 1.0 / np.sqrt(5.0), 1.0])
    deriv = np.zeros((4, 4))
    for i in range(4):
        for j in range(4):
            if i == j:
                deriv[i, j] = sum(1.0 / (nodes[i] - nodes[o]) for o in range(4) if o != i)
            else:
                upper = np.prod([nodes[i] - nodes[o] for o in range(4) if o != i])
                lower = np.prod([nodes[j] - nodes[o] for o in range(4) if o != j])
                deriv[i, j] = upper / (lower * (nodes[i] - nodes[j]))
    return (deriv @ deriv).astype(np.float32)


def tables():
    second = second_table()
    x, y = np.divmod(np.arange(COLS), NY)
    same_x = x[:, None] == x[None, :]
    same_y = y[:, None] == y[None, :]
    same_e = (y[:, None] // 4) == (y[None, :] // 4)
    lap = np.where(same_y, second[x[:, None], x[None, :]], 0.0)
    lap = lap + np.where(same_x & same_e, second[y[:, None] % 4, y[None, :] % 4], 0.0)
    twin = np.where(y % 4 == 0, y - 1, np.where(y % 4 == 3, y + 1, -5))
    pick = np.eye(COLS) + np.where(same_x & (y[None, :] == twin[:, None]), 1.0, 0.0)
    edge = np.zeros((8, COLS))
    for i in range(4):
        edge[i, i * NY] = 1.0
        edge[4 + i, i * NY + NY - 1] = 1.0
    return lap.astype(np.float32), np.concatenate([pick, edge], 0).astype(np.float32)


def split(value):
    high = value.astype(BF16)
    return high, (value - high.astype(F32)).astype(BF16)


def dot(a, b):
    return jnp.dot(a, b, preferred_element_type=F32)


def exact(a, b, dims):
    return lax.dot_general(
        a, b, (dims, ((), ())), precision=lax.Precision.HIGHEST, preferred_element_type=F32
    )


def iota(shape, dim):
    return lax.broadcasted_iota(jnp.int32, shape, dim)


def body(
    n_gx, n_gy,
    state, hyper, pmass, imass, slots, vdiff, frate, cfrac, lap, pick,
    tr, fac,
    v, tsum, acc, edges, xin, yin, cin, small, sl, coef, sent, got, lap_s, pick_s, hyp, dyn,
    in_sem, hs_sem, hr_sem, gs_sem, gr_sem,
):
    per = COLS // n_gx
    half = per // 2
    me = lax.axis_index("gx")
    my = lax.axis_index("gy")
    left, right = lax.rem(me + n_gx - 1, n_gx), lax.rem(me + 1, n_gx)
    down, up = lax.rem(my + n_gy - 1, n_gy), lax.rem(my + 1, n_gy)
    peers = [lax.rem(me + i, n_gx) for i in range(1, n_gx)]
    around = [(left, my), (right, my), (me, down), (me, up),
              (left, down), (left, up), (right, down), (right, up)]

    loads = [
        pltpu.make_async_copy(vdiff.at[0], coef.at[pl.ds(0, LEV)], in_sem.at[0]),
        pltpu.make_async_copy(pmass, small.at[0], in_sem.at[1]),
        pltpu.make_async_copy(imass, small.at[1], in_sem.at[2]),
        pltpu.make_async_copy(lap, lap_s, in_sem.at[3]),
        pltpu.make_async_copy(pick, pick_s, in_sem.at[4]),
        pltpu.make_async_copy(state, v, in_sem.at[5]),
        pltpu.make_async_copy(slots, sl.at[me], in_sem.at[6]),
        pltpu.make_async_copy(frate.at[0], coef.at[pl.ds(2 * LEV, LEV)], in_sem.at[7]),
        pltpu.make_async_copy(cfrac.at[0], coef.at[pl.ds(3 * LEV, LEV)], in_sem.at[8]),
        pltpu.make_async_copy(hyper, hyp.at[0], in_sem.at[9]),
    ]
    for load in loads[1:6]:
        load.start()
    barrier = pltpu.get_barrier_semaphore()
    for target in around[4:] + around[2:4] + [(q, my) for q in peers]:
        pl.semaphore_signal(barrier, inc=1, device_id=target, device_id_type=MESH)
    for load in loads[:1] + loads[6:]:
        load.start()

    rows, lanes = iota((COLS, COLS), 0), iota((COLS, COLS), 1)
    tri = jnp.where(rows < lanes, 1.0, 0.0).astype(BF16)
    level = iota((LEV, COLS), 0)

    def as_row(block):
        return jnp.concatenate([block[x : x + 1, :] for x in range(NX)], axis=1)

    for load in loads[1:5]:
        load.wait()
    mass_row = as_row(small[0])
    inv_row = as_row(small[1])
    inv_col = jnp.sum(jnp.where(rows == lanes, inv_row, 0.0), axis=1, keepdims=True)
    op_high, op_low = split(exact(pick_s[...] * mass_row, lap_s[...], ((1,), (0,))))

    def weigh(r, field):
        high, low = split(field)
        total = dot(op_high, high) + (dot(op_high, low) + dot(op_low, high))
        tsum[r] = total[:COLS]
        for i in range(8):
            edges[r, i] = total[COLS + i : COLS + i + 1]

    def halo(r):
        plan = [
            (tsum.at[r, pl.ds(0, NY)], xin.at[r, 1]),
            (tsum.at[r, pl.ds(COLS - NY, NY)], xin.at[r, 0]),
            (edges.at[r, pl.ds(0, 4)], yin.at[r, 1]),
            (edges.at[r, pl.ds(4, 4)], yin.at[r, 0]),
            (edges.at[r, 0], cin.at[r, 3]),
            (edges.at[r, 4], cin.at[r, 2]),
            (edges.at[r, 3], cin.at[r, 1]),
            (edges.at[r, 7], cin.at[r, 0]),
        ]
        copies = [
            pltpu.make_async_remote_copy(
                src_ref=src, dst_ref=dst, send_sem=hs_sem.at[r, i], recv_sem=hr_sem.at[r, i],
                device_id=around[i], device_id_type=MESH,
            )
            for i, (src, dst) in enumerate(plan)
        ]
        for copy in copies[4:] + copies[2:4] + copies[:2]:
            copy.start()
        return copies

    def assemble(r):
        acc[pl.ds(0, NY), :] = tsum[r, pl.ds(0, NY)] + xin[r, 0]
        acc[pl.ds(NY, COLS - 2 * NY), :] = tsum[r, pl.ds(NY, COLS - 2 * NY)]
        acc[pl.ds(COLS - NY, NY), :] = tsum[r, pl.ds(COLS - NY, NY)] + xin[r, 1]
        corner = {0: (0, 1), 3: (2, 3)}
        for x in range(NX):
            low, high = yin[r, 0, x], yin[r, 1, x]
            if x in corner:
                low = low + cin[r, corner[x][0]]
                high = high + cin[r, corner[x][1]]
            acc[pl.ds(NY * x, 1), :] = acc[pl.ds(NY * x, 1), :] + low
            acc[pl.ds(NY * x + NY - 1, 1), :] = acc[pl.ds(NY * x + NY - 1, 1), :] + high
        return inv_col * acc[...]

    loads[5].wait()
    field = v[...].reshape(COLS, FLD)
    weigh(0, field)

    loads[0].wait()
    diff = coef[pl.ds(0, LEV), :]
    above = jnp.where(level == 0, 0.0, diff)
    below = jnp.where(level == LEV - 1, 0.0, pltpu.roll(diff, LEV - 1, 0))
    surface = jnp.where(level == LEV - 1, diff[0:1], 0.0)
    centre = 1.0 + above + below + surface
    gain = jnp.zeros((1, COLS), F32)
    for k in range(LEV):
        scale = 1.0 / (centre[k : k + 1] - above[k : k + 1] * gain)
        gain = below[k : k + 1] * scale
        coef[pl.ds(LEV + k, 1), :] = scale
    for load in loads[6:9]:
        load.wait()

    pl.semaphore_wait(barrier, n_gx - 1 + 6)

    def exchange(which, box, source):
        copies = [
            pltpu.make_async_remote_copy(
                src_ref=source(q), dst_ref=box.at[me],
                send_sem=gs_sem.at[which], recv_sem=gr_sem.at[which],
                device_id=(q, my), device_id_type=MESH,
            )
            for q in peers
        ]
        for copy in copies:
            copy.start()
        return pltpu.make_async_remote_copy(
            src_ref=box.at[pl.ds(0, n_gx - 1)], dst_ref=box.at[pl.ds(0, n_gx - 1)],
            send_sem=gs_sem.at[which], recv_sem=gr_sem.at[which],
            device_id=(right, my), device_id_type=MESH,
        )

    slot_all = exchange(0, sl, lambda q: sl.at[me])
    first = halo(0)

    own = as_row(sl[me])
    span = own // COLS
    member = jnp.where(span == iota((n_gx, COLS), 0), 1.0, 0.0)
    before = dot(member.astype(BF16), tri)
    rank = jnp.sum(member * before, axis=0, keepdims=True)
    place = span * per + rank.astype(jnp.int32)
    order = jnp.where(rows == place, 1.0, 0.0)
    pair = iota((COLS // 2, COLS), 0)
    pair = (pair // half) * per + pair % half
    order_two = jnp.concatenate(
        [jnp.where(pair == place, 1.0, 0.0), jnp.where(pair + half == place, 1.0, 0.0)], axis=0
    )

    spread = jnp.where(
        iota((COLS, n_gx), 0) // per == iota((COLS, n_gx), 1), 1.0, 0.0
    ).astype(BF16)
    table = coef[...]
    late = table[COLS:].T
    main = table[:COLS].T
    blank = jnp.zeros((COLS, 4 * LEV - COLS), F32)
    rest = jnp.concatenate(
        [jnp.concatenate([late, blank], axis=1), jnp.concatenate([blank, late], axis=1)], axis=0
    )
    slot_all.wait_recv()
    every = jnp.concatenate([sl[:, x, :] for x in range(NX)], axis=1)
    mine = (every // COLS) == me
    before = dot(jnp.where(mine, 1.0, 0.0).astype(BF16), tri)
    ranked = jnp.where(mine, before, -1.0).astype(BF16)
    within = (every % COLS).astype(F32).astype(BF16)
    hit = dot(spread, ranked) == (rows % per).astype(F32)
    chosen = jnp.sum(jnp.where(hit, dot(spread, within), 0.0), axis=1, keepdims=True)
    onehot = jnp.where(chosen == lanes.astype(F32), 1.0, 0.0)
    sent[:, pl.ds(0, per), :] = exact(onehot, main, ((1,), (0,))).reshape(n_gx, per, COLS)
    halves = onehot.reshape(n_gx, 2, half, COLS)
    halves = jnp.concatenate(
        [halves[:, i].reshape(COLS // 2, COLS) for i in range(2)], axis=1
    )
    sent[:, pl.ds(per, half), :] = exact(halves, rest, ((1,), (0,))).reshape(n_gx, half, COLS)
    coef_all = exchange(1, got, lambda q: sent.at[q])
    got[me] = sent[me]

    for copy in first:
        copy.wait_recv()
    weigh(1, assemble(0))
    second = halo(1)

    coef_all.wait_recv()
    box = got[:, pl.ds(0, per), :].reshape(COLS, COLS)
    tail = got[:, pl.ds(per, half), :].reshape(COLS // 2, COLS)
    wide = COLS // 2
    tail = jnp.concatenate([tail[:, :wide], tail[:, wide:]], axis=0)
    early = exact(box, order, ((0,), (0,)))
    late = exact(tail, order_two, ((0,), (0,)))
    diff, scale = early[:LEV], early[LEV : 2 * LEV]
    fall = jnp.concatenate([early[2 * LEV :], late[: 3 * LEV - COLS]], axis=0)
    cloud = late[3 * LEV - COLS :]
    fac[0] = jnp.where(level == 0, 0.0, diff) * scale
    fac[1] = jnp.where(level == LEV - 1, 0.0, pltpu.roll(diff, LEV - 1, 0)) * scale
    fac[2] = scale
    settle = 1.0 / (1.0 + fall)
    fac[3] = settle
    fac[4] = jnp.where(level == 0, 0.0, pltpu.roll(fall, 1, 0)) * settle
    fac[5] = cloud * 0.5

    loads[9].wait()
    for copy in second:
        copy.wait_recv()
    dyn[:, pl.ds(0, FLD)] = v[...].reshape(COLS, FLD) - hyp[...] * assemble(1)
    for j in range(5):
        tr[pl.ds(COLS * j, COLS), :] = dyn[:, pl.ds(COLS * j, COLS)].T
    slot_all.wait_send()
    coef_all.wait_send()
    for copy in first + second:
        copy.wait_send()


def columns(tin, fac, out, tr, wk, rain, res, sem):
    def strided(k):
        return pl.ds(k, VARS, stride=LEV)

    value = jnp.zeros((VARS, COLS), F32)
    for k in range(LEV):
        value = tin[strided(k), :] * fac[2, pl.ds(k, 1), :] + fac[0, pl.ds(k, 1), :] * value
        wk[k] = value
    value = jnp.zeros((VARS, COLS), F32)
    for k in reversed(range(LEV)):
        value = wk[k] + fac[1, pl.ds(k, 1), :] * value
        tr[strided(k), :] = value

    heat, vapour, liquid = (tr[pl.ds(LEV * j, LEV), :] for j in range(3))
    moved = fac[5] * jnp.maximum(vapour - 0.3 * heat, 0.0)
    tr[pl.ds(0, LEV), :] = heat + 2.0 * moved
    tr[pl.ds(LEV, LEV), :] = vapour - moved
    rain[...] = (liquid + moved) * fac[3]
    drop = jnp.zeros((1, COLS), F32)
    for k in range(LEV):
        drop = rain[pl.ds(k, 1), :] + fac[4, pl.ds(k, 1), :] * drop
        tr[pl.ds(2 * LEV + k, 1), :] = drop

    for j in range(5):
        width = min(COLS, FLD - COLS * j)
        part = tr[pl.ds(COLS * j, COLS), :].T[:, :width].reshape(NX, NY, width)
        res[:, :, pl.ds(COLS * j, width)] = part
    store = pltpu.make_async_copy(res, out, sem)
    store.start()
    store.wait()


def solution(mesh):
    n_gx, n_gy = mesh.shape["gx"], mesh.shape["gy"]
    per = COLS // n_gx
    lap, pick = tables()
    anywhere = pl.BlockSpec(memory_space=pl.ANY)
    inside = pl.BlockSpec(memory_space=pltpu.VMEM)
    dma = pltpu.SemaphoreType.DMA

    def local(state, hyper, pmass, imass, slots, vdiff, frate, cfrac):
        fields, factors = pl.pallas_call(
            functools.partial(body, n_gx, n_gy),
            out_shape=(pltpu.VMEM((5 * COLS, COLS), F32), pltpu.VMEM((6, LEV, COLS), F32)),
            in_specs=[anywhere] * 10,
            out_specs=(inside, inside),
            scratch_shapes=[
                pltpu.VMEM((NX, NY, FLD), F32),
                pltpu.VMEM((2, COLS, FLD), F32),
                pltpu.VMEM((COLS, FLD), F32),
                pltpu.VMEM((2, 8, 1, FLD), F32),
                pltpu.VMEM((2, 2, NY, FLD), F32),
                pltpu.VMEM((2, 2, 4, 1, FLD), F32),
                pltpu.VMEM((2, 4, 1, FLD), F32),
                pltpu.VMEM((2, NX, NY), F32),
                pltpu.VMEM((n_gx, NX, NY), jnp.int32),
                pltpu.VMEM((4 * LEV, COLS), F32),
                pltpu.VMEM((n_gx, per + per // 2, COLS), F32),
                pltpu.VMEM((n_gx, per + per // 2, COLS), F32),
                pltpu.VMEM((COLS, COLS), F32),
                pltpu.VMEM((COLS + 8, COLS), F32),
                pltpu.VMEM((1, FLD), F32),
                pltpu.VMEM((COLS, 5 * COLS), F32),
                dma((10,)),
                dma((2, 8)),
                dma((2, 8)),
                dma((2,)),
                dma((2,)),
            ],
            compiler_params=pltpu.CompilerParams(collective_id=0, has_side_effects=True),
        )(state, hyper, pmass, imass, slots, vdiff, frate, cfrac,
          jnp.asarray(lap), jnp.asarray(pick))
        return pl.pallas_call(
            columns,
            out_shape=jax.ShapeDtypeStruct((NX, NY, FLD), F32),
            in_specs=[inside, inside],
            out_specs=anywhere,
            scratch_shapes=[
                pltpu.VMEM((5 * COLS, COLS), F32),
                pltpu.VMEM((LEV, VARS, COLS), F32),
                pltpu.VMEM((LEV, COLS), F32),
                pltpu.VMEM((NX, NY, FLD), F32),
                dma,
            ],
        )(*(pltpu.with_memory_space_constraint(x, pltpu.VMEM) for x in (fields, factors)))

    placed = (
        P("gx", "gy", None), P(), P("gx", "gy"), P("gx", "gy"), P("gx", "gy"),
        P("gy", None, "gx"), P("gy", None, "gx"), P("gy", None, "gx"),
    )
    return jax.shard_map(
        local, mesh=mesh, in_specs=placed, out_specs=P("gx", "gy", None), check_vma=False
    )
```

```python
import functools

import jax
import jax.numpy as jnp
import numpy as np
from jax import lax
from jax.experimental import pallas as pl
from jax.experimental.pallas import tpu as pltpu
from jax.sharding import PartitionSpec as P

MESH = pl.DeviceIdType.MESH
F32 = jnp.float32
BF16 = jnp.bfloat16
NX, NY, COLS, LEV, VARS = 4, 32, 128, 48, 11
Z = 8
FLD = LEV * VARS


def second_table():
    nodes = np.array([-1.0, -1.0 / np.sqrt(5.0), 1.0 / np.sqrt(5.0), 1.0])
    deriv = np.zeros((4, 4))
    for i in range(4):
        for j in range(4):
            if i == j:
                deriv[i, j] = sum(1.0 / (nodes[i] - nodes[o]) for o in range(4) if o != i)
            else:
                upper = np.prod([nodes[i] - nodes[o] for o in range(4) if o != i])
                lower = np.prod([nodes[j] - nodes[o] for o in range(4) if o != j])
                deriv[i, j] = upper / (lower * (nodes[i] - nodes[j]))
    return (deriv @ deriv).astype(np.float32)


def tables():
    second = second_table()
    x, y = np.divmod(np.arange(COLS), NY)
    same_x = x[:, None] == x[None, :]
    same_y = y[:, None] == y[None, :]
    same_e = (y[:, None] // 4) == (y[None, :] // 4)
    lap = np.where(same_y, second[x[:, None], x[None, :]], 0.0)
    lap = lap + np.where(same_x & same_e, second[y[:, None] % 4, y[None, :] % 4], 0.0)
    twin = np.where(y % 4 == 0, y - 1, np.where(y % 4 == 3, y + 1, -5))
    pick = np.eye(COLS) + np.where(same_x & (y[None, :] == twin[:, None]), 1.0, 0.0)
    edge = np.zeros((8, COLS))
    for i in range(4):
        edge[i, i * NY] = 1.0
        edge[4 + i, i * NY + NY - 1] = 1.0
    return lap.astype(np.float32), np.concatenate([pick, edge], 0).astype(np.float32)


def split(value):
    high = value.astype(BF16)
    return high, (value - high.astype(F32)).astype(BF16)


def dot(a, b):
    return jnp.dot(a, b, preferred_element_type=F32)


def exact(a, b, dims):
    return lax.dot_general(
        a, b, (dims, ((), ())), precision=lax.Precision.HIGHEST, preferred_element_type=F32
    )


def iota(shape, dim):
    return lax.broadcasted_iota(jnp.int32, shape, dim)


def body(
    n_gx, n_gy,
    state, hyper, pmass, imass, slots, vdiff, frate, cfrac, lap, pick,
    tr, fac,
    v, tsum, acc, edges, xin, yin, cin, small, sl, coef, sent, got, lap_s, pick_s, hyp, dyn,
    in_sem, hs_sem, hr_sem, gs_sem, gr_sem, here_sem,
):
    per = COLS // n_gx
    half = per // 2
    me = lax.axis_index("gx")
    my = lax.axis_index("gy")
    left, right = lax.rem(me + n_gx - 1, n_gx), lax.rem(me + 1, n_gx)
    down, up = lax.rem(my + n_gy - 1, n_gy), lax.rem(my + 1, n_gy)
    far_first = sorted(range(1, n_gx), key=lambda i: -min(i, n_gx - i))
    peers = [lax.rem(me + i, n_gx) for i in far_first]
    core = lax.rem(me, 2)
    chip = me // 2
    beside = lax.rem(chip + n_gx // 2 - 1 + 2 * core, n_gx // 2)
    around = [(left, my), (right, my), (me, down), (me, up),
              (left, down), (left, up), (right, down), (right, up)]

    loads = [
        pltpu.make_async_copy(vdiff.at[0], coef.at[pl.ds(0, LEV)], in_sem.at[0]),
        pltpu.make_async_copy(pmass, small.at[0], in_sem.at[1]),
        pltpu.make_async_copy(imass, small.at[1], in_sem.at[2]),
        pltpu.make_async_copy(lap, lap_s, in_sem.at[3]),
        pltpu.make_async_copy(pick, pick_s, in_sem.at[4]),
        pltpu.make_async_copy(state, v, in_sem.at[5]),
        pltpu.make_async_copy(slots, sl.at[me], in_sem.at[6]),
        pltpu.make_async_copy(frate.at[0], coef.at[pl.ds(2 * LEV, LEV)], in_sem.at[7]),
        pltpu.make_async_copy(cfrac.at[0], coef.at[pl.ds(3 * LEV, LEV)], in_sem.at[8]),
        pltpu.make_async_copy(hyper, hyp.at[0], in_sem.at[9]),
    ]
    for load in loads[1:6]:
        load.start()
    barrier = pltpu.get_barrier_semaphore()

    def arrive(gx, gy):
        pl.semaphore_signal(barrier, inc=1, device_id=(gx, gy), device_id_type=MESH)

    for gy in (down, up):
        arrive(2 * beside + 1, gy)
        arrive(2 * chip + 1, gy)
    arrive(2 * beside + 1, my)
    for i in sorted(range(1, n_gx // 2), key=lambda i: -min(i, n_gx // 2 - i)):
        arrive(2 * lax.rem(chip + i, n_gx // 2), my)

    @pl.when(core == 0)
    def _():
        arrive(me + 1, my)

    @pl.when(core == 1)
    def _():
        arrive(me - 1, my)

    def ready(counter, amount):
        partner = me + 1 - 2 * core

        @pl.when(core == counter)
        def _():
            pl.semaphore_wait(barrier, amount)
            pl.semaphore_signal(
                here_sem.at[counter], inc=1, device_id=(partner, my), device_id_type=MESH
            )

        @pl.when(core != counter)
        def _():
            pl.semaphore_wait(here_sem.at[counter], 1)

    for load in loads[:1] + loads[6:]:
        load.start()

    rows, lanes = iota((COLS, COLS), 0), iota((COLS, COLS), 1)
    tri = jnp.where(rows < lanes, 1.0, 0.0).astype(BF16)
    level = iota((LEV, COLS), 0)

    def as_row(block):
        return jnp.concatenate([block[x : x + 1, :] for x in range(NX)], axis=1)

    for load in loads[1:5]:
        load.wait()
    mass_row = as_row(small[0])
    inv_row = as_row(small[1])
    inv_col = jnp.sum(jnp.where(rows == lanes, inv_row, 0.0), axis=1, keepdims=True)
    op_high, op_low = split(exact(pick_s[...] * mass_row, lap_s[...], ((1,), (0,))))

    def weigh(r, field):
        high, low = split(field)
        total = dot(op_high, high) + (dot(op_high, low) + dot(op_low, high))
        tsum[r] = total[:COLS]
        for i in range(8):
            edges[r, i] = total[COLS + i : COLS + i + 1]

    def halo(r):
        plan = [
            (tsum.at[r, pl.ds(0, NY)], xin.at[r, 1]),
            (tsum.at[r, pl.ds(COLS - NY, NY)], xin.at[r, 0]),
            (edges.at[r, pl.ds(0, 4)], yin.at[r, 1]),
            (edges.at[r, pl.ds(4, 4)], yin.at[r, 0]),
            (edges.at[r, 0], cin.at[r, 3]),
            (edges.at[r, 4], cin.at[r, 2]),
            (edges.at[r, 3], cin.at[r, 1]),
            (edges.at[r, 7], cin.at[r, 0]),
        ]
        copies = [
            pltpu.make_async_remote_copy(
                src_ref=src, dst_ref=dst, send_sem=hs_sem.at[r, i], recv_sem=hr_sem.at[r, i],
                device_id=around[i], device_id_type=MESH,
            )
            for i, (src, dst) in enumerate(plan)
        ]
        return copies

    def begin(copies):
        for copy in copies[4:] + copies[2:4] + copies[:2]:
            copy.start()

    def assemble(r):
        acc[pl.ds(0, NY), :] = tsum[r, pl.ds(0, NY)] + xin[r, 0]
        acc[pl.ds(NY, COLS - 2 * NY), :] = tsum[r, pl.ds(NY, COLS - 2 * NY)]
        acc[pl.ds(COLS - NY, NY), :] = tsum[r, pl.ds(COLS - NY, NY)] + xin[r, 1]
        corner = {0: (0, 1), 3: (2, 3)}
        for x in range(NX):
            low, high = yin[r, 0, x], yin[r, 1, x]
            if x in corner:
                low = low + cin[r, corner[x][0]]
                high = high + cin[r, corner[x][1]]
            acc[pl.ds(NY * x, 1), :] = acc[pl.ds(NY * x, 1), :] + low
            acc[pl.ds(NY * x + NY - 1, 1), :] = acc[pl.ds(NY * x + NY - 1, 1), :] + high
        return inv_col * acc[...]

    loads[5].wait()
    field = v[...].reshape(COLS, FLD)
    weigh(0, field)

    first, second = halo(0), halo(1)

    def exchange(which, box, source):
        copies = [
            pltpu.make_async_remote_copy(
                src_ref=source(q), dst_ref=box.at[me],
                send_sem=gs_sem.at[which], recv_sem=gr_sem.at[which],
                device_id=(q, my), device_id_type=MESH,
            )
            for q in peers
        ]
        every = pltpu.make_async_remote_copy(
            src_ref=box.at[pl.ds(0, n_gx - 1)], dst_ref=box.at[pl.ds(0, n_gx - 1)],
            send_sem=gs_sem.at[which], recv_sem=gr_sem.at[which],
            device_id=(right, my), device_id_type=MESH,
        )
        return copies, every

    slot_sends, slot_all = exchange(0, sl, lambda q: sl.at[me])
    coef_sends, coef_all = exchange(1, got, lambda q: sent.at[q])

    def pivots():
        diff = coef[pl.ds(0, LEV), :]
        above = jnp.where(level == 0, 0.0, diff)
        below = jnp.where(level == LEV - 1, 0.0, pltpu.roll(diff, LEV - 1, 0))
        surface = jnp.where(level == LEV - 1, diff[0:1], 0.0)
        centre = 1.0 + above + below + surface
        gain = jnp.zeros((1, COLS), F32)
        for k in range(LEV):
            scale = 1.0 / (centre[k : k + 1] - above[k : k + 1] * gain)
            gain = below[k : k + 1] * scale
            coef[pl.ds(LEV + k, 1), :] = scale

    def ask():
        ready(0, n_gx - 1)
        for copy in slot_sends:
            copy.start()

    def answer():
        spread = jnp.where(
            iota((COLS, n_gx), 0) // per == iota((COLS, n_gx), 1), 1.0, 0.0
        ).astype(BF16)
        table = coef[...]
        late = table[COLS:].T
        main = table[:COLS].T
        blank = jnp.zeros((COLS, 4 * LEV - COLS), F32)
        rest = jnp.concatenate(
            [jnp.concatenate([late, blank], axis=1), jnp.concatenate([blank, late], axis=1)],
            axis=0,
        )
        slot_all.wait_recv()
        every = jnp.concatenate([sl[:, x, :] for x in range(NX)], axis=1)
        mine = (every // COLS) == me
        before = dot(jnp.where(mine, 1.0, 0.0).astype(BF16), tri)
        ranked = jnp.where(mine, before, -1.0).astype(BF16)
        within = (every % COLS).astype(F32).astype(BF16)
        hit = dot(spread, ranked) == (rows % per).astype(F32)
        chosen = jnp.sum(jnp.where(hit, dot(spread, within), 0.0), axis=1, keepdims=True)
        onehot = jnp.where(chosen == lanes.astype(F32), 1.0, 0.0)
        sent[:, pl.ds(0, per), :] = exact(onehot, main, ((1,), (0,))).reshape(n_gx, per, COLS)
        halves = onehot.reshape(n_gx, 2, half, COLS)
        halves = jnp.concatenate(
            [halves[:, i].reshape(COLS // 2, COLS) for i in range(2)], axis=1
        )
        sent[:, pl.ds(per, half), :] = exact(halves, rest, ((1,), (0,))).reshape(n_gx, half, COLS)
        for copy in coef_sends:
            copy.start()
        got[me] = sent[me]

    def pass_edges():
        ready(1, 11)
        begin(first)

    def pass_again():
        for copy in first:
            copy.wait_recv()
        weigh(1, assemble(0))
        begin(second)

    for load in loads[:1] + loads[6:9]:
        load.wait()
    early = lax.rem(my, Z) < 2

    @pl.when(early)
    def _():
        pivots()
        ask()
        answer()

    pass_edges()

    @pl.when(jnp.logical_not(early))
    def _():
        pivots()
        ask()

    pass_again()

    @pl.when(jnp.logical_not(early))
    def _():
        answer()

    own = as_row(sl[me])
    span = own // COLS
    member = jnp.where(span == iota((n_gx, COLS), 0), 1.0, 0.0)
    before = dot(member.astype(BF16), tri)
    rank = jnp.sum(member * before, axis=0, keepdims=True)
    place = span * per + rank.astype(jnp.int32)
    order = jnp.where(rows == place, 1.0, 0.0)
    pair = iota((COLS // 2, COLS), 0)
    pair = (pair // half) * per + pair % half
    order_two = jnp.concatenate(
        [jnp.where(pair == place, 1.0, 0.0), jnp.where(pair + half == place, 1.0, 0.0)], axis=0
    )

    coef_all.wait_recv()
    box = got[:, pl.ds(0, per), :].reshape(COLS, COLS)
    tail = got[:, pl.ds(per, half), :].reshape(COLS // 2, COLS)
    wide = COLS // 2
    tail = jnp.concatenate([tail[:, :wide], tail[:, wide:]], axis=0)
    early = exact(box, order, ((0,), (0,)))
    late = exact(tail, order_two, ((0,), (0,)))
    diff, scale = early[:LEV], early[LEV : 2 * LEV]
    fall = jnp.concatenate([early[2 * LEV :], late[: 3 * LEV - COLS]], axis=0)
    cloud = late[3 * LEV - COLS :]
    fac[0] = jnp.where(level == 0, 0.0, diff) * scale
    fac[1] = jnp.where(level == LEV - 1, 0.0, pltpu.roll(diff, LEV - 1, 0)) * scale
    fac[2] = scale
    settle = 1.0 / (1.0 + fall)
    fac[3] = settle
    fac[4] = jnp.where(level == 0, 0.0, pltpu.roll(fall, 1, 0)) * settle
    fac[5] = cloud * 0.5

    loads[9].wait()
    for copy in second:
        copy.wait_recv()
    dyn[:, pl.ds(0, FLD)] = v[...].reshape(COLS, FLD) - hyp[...] * assemble(1)
    for j in range(5):
        tr[pl.ds(COLS * j, COLS), :] = dyn[:, pl.ds(COLS * j, COLS)].T
    slot_all.wait_send()
    coef_all.wait_send()
    for copy in first + second:
        copy.wait_send()


def columns(tin, fac, out, tr, wk, rain, res, sem):
    def strided(k):
        return pl.ds(k, VARS, stride=LEV)

    value = jnp.zeros((VARS, COLS), F32)
    for k in range(LEV):
        value = tin[strided(k), :] * fac[2, pl.ds(k, 1), :] + fac[0, pl.ds(k, 1), :] * value
        wk[k] = value
    value = jnp.zeros((VARS, COLS), F32)
    for k in reversed(range(LEV)):
        value = wk[k] + fac[1, pl.ds(k, 1), :] * value
        tr[strided(k), :] = value

    heat, vapour, liquid = (tr[pl.ds(LEV * j, LEV), :] for j in range(3))
    moved = fac[5] * jnp.maximum(vapour - 0.3 * heat, 0.0)
    tr[pl.ds(0, LEV), :] = heat + 2.0 * moved
    tr[pl.ds(LEV, LEV), :] = vapour - moved
    rain[...] = (liquid + moved) * fac[3]
    drop = jnp.zeros((1, COLS), F32)
    for k in range(LEV):
        drop = rain[pl.ds(k, 1), :] + fac[4, pl.ds(k, 1), :] * drop
        tr[pl.ds(2 * LEV + k, 1), :] = drop

    for j in range(5):
        width = min(COLS, FLD - COLS * j)
        part = tr[pl.ds(COLS * j, COLS), :].T[:, :width].reshape(NX, NY, width)
        res[:, :, pl.ds(COLS * j, width)] = part
    store = pltpu.make_async_copy(res, out, sem)
    store.start()
    store.wait()


def solution(mesh):
    n_gx, n_gy = mesh.shape["gx"], mesh.shape["gy"]
    per = COLS // n_gx
    lap, pick = tables()
    anywhere = pl.BlockSpec(memory_space=pl.ANY)
    inside = pl.BlockSpec(memory_space=pltpu.VMEM)
    dma = pltpu.SemaphoreType.DMA

    def local(state, hyper, pmass, imass, slots, vdiff, frate, cfrac):
        fields, factors = pl.pallas_call(
            functools.partial(body, n_gx, n_gy),
            out_shape=(pltpu.VMEM((5 * COLS, COLS), F32), pltpu.VMEM((6, LEV, COLS), F32)),
            in_specs=[anywhere] * 10,
            out_specs=(inside, inside),
            scratch_shapes=[
                pltpu.VMEM((NX, NY, FLD), F32),
                pltpu.VMEM((2, COLS, FLD), F32),
                pltpu.VMEM((COLS, FLD), F32),
                pltpu.VMEM((2, 8, 1, FLD), F32),
                pltpu.VMEM((2, 2, NY, FLD), F32),
                pltpu.VMEM((2, 2, 4, 1, FLD), F32),
                pltpu.VMEM((2, 4, 1, FLD), F32),
                pltpu.VMEM((2, NX, NY), F32),
                pltpu.VMEM((n_gx, NX, NY), jnp.int32),
                pltpu.VMEM((4 * LEV, COLS), F32),
                pltpu.VMEM((n_gx, per + per // 2, COLS), F32),
                pltpu.VMEM((n_gx, per + per // 2, COLS), F32),
                pltpu.VMEM((COLS, COLS), F32),
                pltpu.VMEM((COLS + 8, COLS), F32),
                pltpu.VMEM((1, FLD), F32),
                pltpu.VMEM((COLS, 5 * COLS), F32),
                dma((10,)),
                dma((2, 8)),
                dma((2, 8)),
                dma((2,)),
                dma((2,)),
                pltpu.SemaphoreType.REGULAR((2,)),
            ],
            compiler_params=pltpu.CompilerParams(collective_id=0, has_side_effects=True),
        )(state, hyper, pmass, imass, slots, vdiff, frate, cfrac,
          jnp.asarray(lap), jnp.asarray(pick))
        return pl.pallas_call(
            columns,
            out_shape=jax.ShapeDtypeStruct((NX, NY, FLD), F32),
            in_specs=[inside, inside],
            out_specs=anywhere,
            scratch_shapes=[
                pltpu.VMEM((5 * COLS, COLS), F32),
                pltpu.VMEM((LEV, VARS, COLS), F32),
                pltpu.VMEM((LEV, COLS), F32),
                pltpu.VMEM((NX, NY, FLD), F32),
                dma,
            ],
        )(*(pltpu.with_memory_space_constraint(x, pltpu.VMEM) for x in (fields, factors)))

    placed = (
        P("gx", "gy", None), P(), P("gx", "gy"), P("gx", "gy"), P("gx", "gy"),
        P("gy", None, "gx"), P("gy", None, "gx"), P("gy", None, "gx"),
    )
    return jax.shard_map(
        local, mesh=mesh, in_specs=placed, out_specs=P("gx", "gy", None), check_vma=False
    )
```

```python
import functools

import jax
import jax.numpy as jnp
import numpy as np
from jax import lax
from jax.experimental import pallas as pl
from jax.experimental.pallas import tpu as pltpu
from jax.sharding import PartitionSpec as P

MESH = pl.DeviceIdType.MESH
F32 = jnp.float32
BF16 = jnp.bfloat16
NX, NY, COLS, LEV, VARS = 4, 32, 128, 48, 11
Z = 8
FLD = LEV * VARS


def second_table():
    nodes = np.array([-1.0, -1.0 / np.sqrt(5.0), 1.0 / np.sqrt(5.0), 1.0])
    deriv = np.zeros((4, 4))
    for i in range(4):
        for j in range(4):
            if i == j:
                deriv[i, j] = sum(1.0 / (nodes[i] - nodes[o]) for o in range(4) if o != i)
            else:
                upper = np.prod([nodes[i] - nodes[o] for o in range(4) if o != i])
                lower = np.prod([nodes[j] - nodes[o] for o in range(4) if o != j])
                deriv[i, j] = upper / (lower * (nodes[i] - nodes[j]))
    return (deriv @ deriv).astype(np.float32)


def tables():
    second = second_table()
    x, y = np.divmod(np.arange(COLS), NY)
    same_x = x[:, None] == x[None, :]
    same_y = y[:, None] == y[None, :]
    same_e = (y[:, None] // 4) == (y[None, :] // 4)
    lap = np.where(same_y, second[x[:, None], x[None, :]], 0.0)
    lap = lap + np.where(same_x & same_e, second[y[:, None] % 4, y[None, :] % 4], 0.0)
    twin = np.where(y % 4 == 0, y - 1, np.where(y % 4 == 3, y + 1, -5))
    pick = np.eye(COLS) + np.where(same_x & (y[None, :] == twin[:, None]), 1.0, 0.0)
    edge = np.zeros((8, COLS))
    for i in range(4):
        edge[i, i * NY] = 1.0
        edge[4 + i, i * NY + NY - 1] = 1.0
    return lap.astype(np.float32), np.concatenate([pick, edge], 0).astype(np.float32)


def split(value):
    high = value.astype(BF16)
    return high, (value - high.astype(F32)).astype(BF16)


def dot(a, b):
    return jnp.dot(a, b, preferred_element_type=F32)


def exact(a, b, dims):
    return lax.dot_general(
        a, b, (dims, ((), ())), precision=lax.Precision.HIGHEST, preferred_element_type=F32
    )


def iota(shape, dim):
    return lax.broadcasted_iota(jnp.int32, shape, dim)


def body(
    n_gx, n_gy,
    state, hyper, pmass, imass, slots, vdiff, frate, cfrac, lap, pick,
    tr, fac,
    v, tsum, acc, edges, xin, yin, cin, small, sl, coef, sent, got, lap_s, pick_s, hyp, dyn,
    in_sem, hs_sem, hr_sem, gs_sem, gr_sem, here_sem,
):
    per = COLS // n_gx
    half = per // 2
    me = lax.axis_index("gx")
    my = lax.axis_index("gy")
    left, right = lax.rem(me + n_gx - 1, n_gx), lax.rem(me + 1, n_gx)
    down, up = lax.rem(my + n_gy - 1, n_gy), lax.rem(my + 1, n_gy)
    far_first = sorted(range(1, n_gx), key=lambda i: -min(i, n_gx - i))
    peers = [lax.rem(me + i, n_gx) for i in far_first]
    core = lax.rem(me, 2)
    chip = me // 2
    beside = lax.rem(chip + n_gx // 2 - 1 + 2 * core, n_gx // 2)
    around = [(left, my), (right, my), (me, down), (me, up),
              (left, down), (left, up), (right, down), (right, up)]

    loads = [
        pltpu.make_async_copy(vdiff.at[0], coef.at[pl.ds(0, LEV)], in_sem.at[0]),
        pltpu.make_async_copy(pmass, small.at[0], in_sem.at[1]),
        pltpu.make_async_copy(imass, small.at[1], in_sem.at[2]),
        pltpu.make_async_copy(lap, lap_s, in_sem.at[3]),
        pltpu.make_async_copy(pick, pick_s, in_sem.at[4]),
        pltpu.make_async_copy(state, v, in_sem.at[5]),
        pltpu.make_async_copy(slots, sl.at[me], in_sem.at[6]),
        pltpu.make_async_copy(frate.at[0], coef.at[pl.ds(2 * LEV, LEV)], in_sem.at[7]),
        pltpu.make_async_copy(cfrac.at[0], coef.at[pl.ds(3 * LEV, LEV)], in_sem.at[8]),
        pltpu.make_async_copy(hyper, hyp.at[0], in_sem.at[9]),
    ]
    for load in loads[1:6]:
        load.start()
    barrier = pltpu.get_barrier_semaphore()

    def arrive(gx, gy):
        pl.semaphore_signal(barrier, inc=1, device_id=(gx, gy), device_id_type=MESH)

    for gy in (down, up):
        arrive(2 * beside + 1, gy)
        arrive(2 * chip + 1, gy)
    arrive(2 * beside + 1, my)
    for i in sorted(range(1, n_gx // 2), key=lambda i: -min(i, n_gx // 2 - i)):
        arrive(2 * lax.rem(chip + i, n_gx // 2), my)

    @pl.when(core == 0)
    def _():
        arrive(me + 1, my)

    @pl.when(core == 1)
    def _():
        arrive(me - 1, my)

    def ready(counter, amount):
        partner = me + 1 - 2 * core

        @pl.when(core == counter)
        def _():
            pl.semaphore_wait(barrier, amount)
            pl.semaphore_signal(
                here_sem.at[counter], inc=1, device_id=(partner, my), device_id_type=MESH
            )

        @pl.when(core != counter)
        def _():
            pl.semaphore_wait(here_sem.at[counter], 1)

    for load in loads[:1] + loads[6:]:
        load.start()

    rows, lanes = iota((COLS, COLS), 0), iota((COLS, COLS), 1)
    tri = jnp.where(rows < lanes, 1.0, 0.0).astype(BF16)
    level = iota((LEV, COLS), 0)

    def as_row(block):
        return jnp.concatenate([block[x : x + 1, :] for x in range(NX)], axis=1)

    for load in loads[1:5]:
        load.wait()
    mass_row = as_row(small[0])
    inv_row = as_row(small[1])
    inv_col = jnp.sum(jnp.where(rows == lanes, inv_row, 0.0), axis=1, keepdims=True)
    pick_high, pick_low = split(pick_s[...] * mass_row)
    lap_high, lap_low = split(lap_s[...])
    op_high, op_low = split(
        dot(
            jnp.concatenate([pick_high, pick_high], axis=1),
            jnp.concatenate([lap_high, lap_low], axis=0),
        )
        + dot(pick_low, lap_high)
    )
    op_twice = jnp.concatenate([op_high, op_high], axis=1)

    def weigh(r, field):
        high, low = split(field)
        total = dot(op_twice, jnp.concatenate([high, low], axis=0)) + dot(op_low, high)
        tsum[r] = total[:COLS]
        for i in range(8):
            edges[r, i] = total[COLS + i : COLS + i + 1]

    def halo(r):
        plan = [
            (tsum.at[r, pl.ds(0, NY)], xin.at[r, 1]),
            (tsum.at[r, pl.ds(COLS - NY, NY)], xin.at[r, 0]),
            (edges.at[r, pl.ds(0, 4)], yin.at[r, 1]),
            (edges.at[r, pl.ds(4, 4)], yin.at[r, 0]),
            (edges.at[r, 0], cin.at[r, 3]),
            (edges.at[r, 4], cin.at[r, 2]),
            (edges.at[r, 3], cin.at[r, 1]),
            (edges.at[r, 7], cin.at[r, 0]),
        ]
        copies = [
            pltpu.make_async_remote_copy(
                src_ref=src, dst_ref=dst, send_sem=hs_sem.at[r, i], recv_sem=hr_sem.at[r, i],
                device_id=around[i], device_id_type=MESH,
            )
            for i, (src, dst) in enumerate(plan)
        ]
        return copies

    def begin(copies):
        for copy in copies[4:] + copies[2:4] + copies[:2]:
            copy.start()

    def assemble(r):
        acc[pl.ds(0, NY), :] = tsum[r, pl.ds(0, NY)] + xin[r, 0]
        acc[pl.ds(NY, COLS - 2 * NY), :] = tsum[r, pl.ds(NY, COLS - 2 * NY)]
        acc[pl.ds(COLS - NY, NY), :] = tsum[r, pl.ds(COLS - NY, NY)] + xin[r, 1]
        corner = {0: (0, 1), 3: (2, 3)}
        for x in range(NX):
            low, high = yin[r, 0, x], yin[r, 1, x]
            if x in corner:
                low = low + cin[r, corner[x][0]]
                high = high + cin[r, corner[x][1]]
            acc[pl.ds(NY * x, 1), :] = acc[pl.ds(NY * x, 1), :] + low
            acc[pl.ds(NY * x + NY - 1, 1), :] = acc[pl.ds(NY * x + NY - 1, 1), :] + high
        return inv_col * acc[...]

    loads[5].wait()
    field = v[...].reshape(COLS, FLD)
    weigh(0, field)

    first, second = halo(0), halo(1)

    def exchange(which, box, source):
        copies = [
            pltpu.make_async_remote_copy(
                src_ref=source(q), dst_ref=box.at[me],
                send_sem=gs_sem.at[which], recv_sem=gr_sem.at[which],
                device_id=(q, my), device_id_type=MESH,
            )
            for q in peers
        ]
        every = pltpu.make_async_remote_copy(
            src_ref=box.at[pl.ds(0, n_gx - 1)], dst_ref=box.at[pl.ds(0, n_gx - 1)],
            send_sem=gs_sem.at[which], recv_sem=gr_sem.at[which],
            device_id=(right, my), device_id_type=MESH,
        )
        return copies, every

    slot_sends, slot_all = exchange(0, sl, lambda q: sl.at[me])
    coef_sends, coef_all = exchange(1, got, lambda q: sent.at[q])

    def pivots():
        diff = coef[pl.ds(0, LEV), :]
        above = jnp.where(level == 0, 0.0, diff)
        below = jnp.where(level == LEV - 1, 0.0, pltpu.roll(diff, LEV - 1, 0))
        surface = jnp.where(level == LEV - 1, diff[0:1], 0.0)
        centre = 1.0 + above + below + surface
        gain = jnp.zeros((1, COLS), F32)
        for k in range(LEV):
            scale = 1.0 / (centre[k : k + 1] - above[k : k + 1] * gain)
            gain = below[k : k + 1] * scale
            coef[pl.ds(LEV + k, 1), :] = scale

    def ask():
        ready(0, n_gx - 1)
        for copy in slot_sends:
            copy.start()

    def answer():
        spread = jnp.where(
            iota((COLS, n_gx), 0) // per == iota((COLS, n_gx), 1), 1.0, 0.0
        ).astype(BF16)
        table = coef[...]
        late = table[COLS:].T
        main = table[:COLS].T
        blank = jnp.zeros((COLS, 4 * LEV - COLS), F32)
        rest = jnp.concatenate(
            [jnp.concatenate([late, blank], axis=1), jnp.concatenate([blank, late], axis=1)],
            axis=0,
        )
        slot_all.wait_recv()
        every = jnp.concatenate([sl[:, x, :] for x in range(NX)], axis=1)
        mine = (every // COLS) == me
        before = dot(jnp.where(mine, 1.0, 0.0).astype(BF16), tri)
        ranked = jnp.where(mine, before, -1.0).astype(BF16)
        within = (every % COLS).astype(F32).astype(BF16)
        hit = dot(spread, ranked) == (rows % per).astype(F32)
        chosen = jnp.sum(jnp.where(hit, dot(spread, within), 0.0), axis=1, keepdims=True)
        onehot = jnp.where(chosen == lanes.astype(F32), 1.0, 0.0)
        sent[:, pl.ds(0, per), :] = exact(onehot, main, ((1,), (0,))).reshape(n_gx, per, COLS)
        halves = onehot.reshape(n_gx, 2, half, COLS)
        halves = jnp.concatenate(
            [halves[:, i].reshape(COLS // 2, COLS) for i in range(2)], axis=1
        )
        sent[:, pl.ds(per, half), :] = exact(halves, rest, ((1,), (0,))).reshape(n_gx, half, COLS)
        for copy in coef_sends:
            copy.start()
        got[me] = sent[me]

    def pass_edges():
        ready(1, 11)
        begin(first)

    def pass_again():
        for copy in first:
            copy.wait_recv()
        weigh(1, assemble(0))
        begin(second)

    for load in loads[:1] + loads[6:9]:
        load.wait()
    early = lax.rem(my, Z) < 2

    @pl.when(early)
    def _():
        pivots()
        ask()

    pass_edges()

    @pl.when(early)
    def _():
        answer()

    @pl.when(jnp.logical_not(early))
    def _():
        pivots()
        ask()

    pass_again()

    @pl.when(jnp.logical_not(early))
    def _():
        answer()

    own = as_row(sl[me])
    span = own // COLS
    member = jnp.where(span == iota((n_gx, COLS), 0), 1.0, 0.0)
    before = dot(member.astype(BF16), tri)
    rank = jnp.sum(member * before, axis=0, keepdims=True)
    place = span * per + rank.astype(jnp.int32)
    order = jnp.where(rows == place, 1.0, 0.0)
    pair = iota((COLS // 2, COLS), 0)
    pair = (pair // half) * per + pair % half
    order_two = jnp.concatenate(
        [jnp.where(pair == place, 1.0, 0.0), jnp.where(pair + half == place, 1.0, 0.0)], axis=0
    )

    coef_all.wait_recv()
    box = got[:, pl.ds(0, per), :].reshape(COLS, COLS)
    tail = got[:, pl.ds(per, half), :].reshape(COLS // 2, COLS)
    wide = COLS // 2
    tail = jnp.concatenate([tail[:, :wide], tail[:, wide:]], axis=0)
    early = exact(box, order, ((0,), (0,)))
    late = exact(tail, order_two, ((0,), (0,)))
    diff, scale = early[:LEV], early[LEV : 2 * LEV]
    fall = jnp.concatenate([early[2 * LEV :], late[: 3 * LEV - COLS]], axis=0)
    cloud = late[3 * LEV - COLS :]
    fac[0] = jnp.where(level == 0, 0.0, diff) * scale
    fac[1] = jnp.where(level == LEV - 1, 0.0, pltpu.roll(diff, LEV - 1, 0)) * scale
    fac[2] = scale
    settle = 1.0 / (1.0 + fall)
    fac[3] = settle
    fac[4] = jnp.where(level == 0, 0.0, pltpu.roll(fall, 1, 0)) * settle
    fac[5] = cloud * 0.5

    loads[9].wait()
    for copy in second:
        copy.wait_recv()
    dyn[:, pl.ds(0, FLD)] = v[...].reshape(COLS, FLD) - hyp[...] * assemble(1)
    for j in range(5):
        tr[pl.ds(COLS * j, COLS), :] = dyn[:, pl.ds(COLS * j, COLS)].T
    slot_all.wait_send()
    coef_all.wait_send()
    for copy in first + second:
        copy.wait_send()


def columns(tin, fac, out, tr, wk, rain, res, sem):
    def strided(k):
        return pl.ds(k, VARS, stride=LEV)

    value = jnp.zeros((VARS, COLS), F32)
    for k in range(LEV):
        value = tin[strided(k), :] * fac[2, pl.ds(k, 1), :] + fac[0, pl.ds(k, 1), :] * value
        wk[k] = value
    value = jnp.zeros((VARS, COLS), F32)
    for k in reversed(range(LEV)):
        value = wk[k] + fac[1, pl.ds(k, 1), :] * value
        tr[strided(k), :] = value

    heat, vapour, liquid = (tr[pl.ds(LEV * j, LEV), :] for j in range(3))
    moved = fac[5] * jnp.maximum(vapour - 0.3 * heat, 0.0)
    tr[pl.ds(0, LEV), :] = heat + 2.0 * moved
    tr[pl.ds(LEV, LEV), :] = vapour - moved
    rain[...] = (liquid + moved) * fac[3]
    drop = jnp.zeros((1, COLS), F32)
    for k in range(LEV):
        drop = rain[pl.ds(k, 1), :] + fac[4, pl.ds(k, 1), :] * drop
        tr[pl.ds(2 * LEV + k, 1), :] = drop

    for j in range(5):
        width = min(COLS, FLD - COLS * j)
        part = tr[pl.ds(COLS * j, COLS), :].T[:, :width].reshape(NX, NY, width)
        res[:, :, pl.ds(COLS * j, width)] = part
    store = pltpu.make_async_copy(res, out, sem)
    store.start()
    store.wait()


def solution(mesh):
    n_gx, n_gy = mesh.shape["gx"], mesh.shape["gy"]
    per = COLS // n_gx
    lap, pick = tables()
    anywhere = pl.BlockSpec(memory_space=pl.ANY)
    inside = pl.BlockSpec(memory_space=pltpu.VMEM)
    dma = pltpu.SemaphoreType.DMA

    def local(state, hyper, pmass, imass, slots, vdiff, frate, cfrac):
        fields, factors = pl.pallas_call(
            functools.partial(body, n_gx, n_gy),
            out_shape=(pltpu.VMEM((5 * COLS, COLS), F32), pltpu.VMEM((6, LEV, COLS), F32)),
            in_specs=[anywhere] * 10,
            out_specs=(inside, inside),
            scratch_shapes=[
                pltpu.VMEM((NX, NY, FLD), F32),
                pltpu.VMEM((2, COLS, FLD), F32),
                pltpu.VMEM((COLS, FLD), F32),
                pltpu.VMEM((2, 8, 1, FLD), F32),
                pltpu.VMEM((2, 2, NY, FLD), F32),
                pltpu.VMEM((2, 2, 4, 1, FLD), F32),
                pltpu.VMEM((2, 4, 1, FLD), F32),
                pltpu.VMEM((2, NX, NY), F32),
                pltpu.VMEM((n_gx, NX, NY), jnp.int32),
                pltpu.VMEM((4 * LEV, COLS), F32),
                pltpu.VMEM((n_gx, per + per // 2, COLS), F32),
                pltpu.VMEM((n_gx, per + per // 2, COLS), F32),
                pltpu.VMEM((COLS, COLS), F32),
                pltpu.VMEM((COLS + 8, COLS), F32),
                pltpu.VMEM((1, FLD), F32),
                pltpu.VMEM((COLS, 5 * COLS), F32),
                dma((10,)),
                dma((2, 8)),
                dma((2, 8)),
                dma((2,)),
                dma((2,)),
                pltpu.SemaphoreType.REGULAR((2,)),
            ],
            compiler_params=pltpu.CompilerParams(collective_id=0, has_side_effects=True),
        )(state, hyper, pmass, imass, slots, vdiff, frate, cfrac,
          jnp.asarray(lap), jnp.asarray(pick))
        return pl.pallas_call(
            columns,
            out_shape=jax.ShapeDtypeStruct((NX, NY, FLD), F32),
            in_specs=[inside, inside],
            out_specs=anywhere,
            scratch_shapes=[
                pltpu.VMEM((5 * COLS, COLS), F32),
                pltpu.VMEM((LEV, VARS, COLS), F32),
                pltpu.VMEM((LEV, COLS), F32),
                pltpu.VMEM((NX, NY, FLD), F32),
                dma,
            ],
        )(*(pltpu.with_memory_space_constraint(x, pltpu.VMEM) for x in (fields, factors)))

    placed = (
        P("gx", "gy", None), P(), P("gx", "gy"), P("gx", "gy"), P("gx", "gy"),
        P("gy", None, "gx"), P("gy", None, "gx"), P("gy", None, "gx"),
    )
    return jax.shard_map(
        local, mesh=mesh, in_specs=placed, out_specs=P("gx", "gy", None), check_vma=False
    )
```

```python
import functools

import jax
import jax.numpy as jnp
import numpy as np
from jax import lax
from jax.experimental import pallas as pl
from jax.experimental.pallas import tpu as pltpu
from jax.sharding import PartitionSpec as P

MESH = pl.DeviceIdType.MESH
F32 = jnp.float32
BF16 = jnp.bfloat16
NX, NY, COLS, LEV, VARS = 4, 32, 128, 48, 11
Z = 8
RUN = 8
RUNS = LEV // RUN
FLD = LEV * VARS


def second_table():
    nodes = np.array([-1.0, -1.0 / np.sqrt(5.0), 1.0 / np.sqrt(5.0), 1.0])
    deriv = np.zeros((4, 4))
    for i in range(4):
        for j in range(4):
            if i == j:
                deriv[i, j] = sum(1.0 / (nodes[i] - nodes[o]) for o in range(4) if o != i)
            else:
                upper = np.prod([nodes[i] - nodes[o] for o in range(4) if o != i])
                lower = np.prod([nodes[j] - nodes[o] for o in range(4) if o != j])
                deriv[i, j] = upper / (lower * (nodes[i] - nodes[j]))
    return (deriv @ deriv).astype(np.float32)


def tables():
    second = second_table()
    x, y = np.divmod(np.arange(COLS), NY)
    same_x = x[:, None] == x[None, :]
    same_y = y[:, None] == y[None, :]
    same_e = (y[:, None] // 4) == (y[None, :] // 4)
    lap = np.where(same_y, second[x[:, None], x[None, :]], 0.0)
    lap = lap + np.where(same_x & same_e, second[y[:, None] % 4, y[None, :] % 4], 0.0)
    twin = np.where(y % 4 == 0, y - 1, np.where(y % 4 == 3, y + 1, -5))
    pick = np.eye(COLS) + np.where(same_x & (y[None, :] == twin[:, None]), 1.0, 0.0)
    edge = np.zeros((8, COLS))
    for i in range(4):
        edge[i, i * NY] = 1.0
        edge[4 + i, i * NY + NY - 1] = 1.0
    return lap.astype(np.float32), np.concatenate([pick, edge], 0).astype(np.float32)


def split(value):
    high = value.astype(BF16)
    return high, (value - high.astype(F32)).astype(BF16)


def dot(a, b):
    return jnp.dot(a, b, preferred_element_type=F32)


def exact(a, b, dims):
    return lax.dot_general(
        a, b, (dims, ((), ())), precision=lax.Precision.HIGHEST, preferred_element_type=F32
    )


def iota(shape, dim):
    return lax.broadcasted_iota(jnp.int32, shape, dim)


def body(
    n_gx, n_gy,
    state, hyper, pmass, imass, slots, vdiff, frate, cfrac, lap, pick,
    tr, fac,
    v, tsum, acc, edges, xin, yin, cin, small, sl, coef, sent, got, lap_s, pick_s, hyp, dyn,
    in_sem, hs_sem, hr_sem, gs_sem, gr_sem, here_sem,
):
    per = COLS // n_gx
    half = per // 2
    me = lax.axis_index("gx")
    my = lax.axis_index("gy")
    left, right = lax.rem(me + n_gx - 1, n_gx), lax.rem(me + 1, n_gx)
    down, up = lax.rem(my + n_gy - 1, n_gy), lax.rem(my + 1, n_gy)
    far_first = sorted(range(1, n_gx), key=lambda i: -min(i, n_gx - i))
    peers = [lax.rem(me + i, n_gx) for i in far_first]
    core = lax.rem(me, 2)
    chip = me // 2
    beside = lax.rem(chip + n_gx // 2 - 1 + 2 * core, n_gx // 2)
    around = [(left, my), (right, my), (me, down), (me, up),
              (left, down), (left, up), (right, down), (right, up)]

    loads = [
        pltpu.make_async_copy(vdiff.at[0], coef.at[pl.ds(0, LEV)], in_sem.at[0]),
        pltpu.make_async_copy(pmass, small.at[0], in_sem.at[1]),
        pltpu.make_async_copy(imass, small.at[1], in_sem.at[2]),
        pltpu.make_async_copy(lap, lap_s, in_sem.at[3]),
        pltpu.make_async_copy(pick, pick_s, in_sem.at[4]),
        pltpu.make_async_copy(state, v, in_sem.at[5]),
        pltpu.make_async_copy(slots, sl.at[me], in_sem.at[6]),
        pltpu.make_async_copy(frate.at[0], coef.at[pl.ds(2 * LEV, LEV)], in_sem.at[7]),
        pltpu.make_async_copy(cfrac.at[0], coef.at[pl.ds(3 * LEV, LEV)], in_sem.at[8]),
        pltpu.make_async_copy(hyper, hyp.at[0], in_sem.at[9]),
    ]
    for load in loads[5:6] + loads[1:5]:
        load.start()
    barrier = pltpu.get_barrier_semaphore()

    def arrive(gx, gy):
        pl.semaphore_signal(barrier, inc=1, device_id=(gx, gy), device_id_type=MESH)

    for gy in (down, up):
        arrive(2 * beside + 1, gy)
        arrive(2 * chip + 1, gy)
    arrive(2 * beside + 1, my)
    for i in sorted(range(1, n_gx // 2), key=lambda i: -min(i, n_gx // 2 - i)):
        arrive(2 * lax.rem(chip + i, n_gx // 2), my)

    @pl.when(core == 0)
    def _():
        arrive(me + 1, my)

    @pl.when(core == 1)
    def _():
        arrive(me - 1, my)

    def ready(counter, amount):
        partner = me + 1 - 2 * core

        @pl.when(core == counter)
        def _():
            pl.semaphore_wait(barrier, amount)
            pl.semaphore_signal(
                here_sem.at[counter], inc=1, device_id=(partner, my), device_id_type=MESH
            )

        @pl.when(core != counter)
        def _():
            pl.semaphore_wait(here_sem.at[counter], 1)

    for load in loads[:1] + loads[6:]:
        load.start()

    rows, lanes = iota((COLS, COLS), 0), iota((COLS, COLS), 1)
    tri = jnp.where(rows < lanes, 1.0, 0.0).astype(BF16)
    level = iota((LEV, COLS), 0)

    def as_row(block):
        return jnp.concatenate([block[x : x + 1, :] for x in range(NX)], axis=1)

    for load in loads[1:5]:
        load.wait()
    mass_row = as_row(small[0])
    inv_row = as_row(small[1])
    inv_col = jnp.sum(jnp.where(rows == lanes, inv_row, 0.0), axis=1, keepdims=True)
    pick_high, pick_low = split(pick_s[...] * mass_row)
    lap_high, lap_low = split(lap_s[...])
    op_high, op_low = split(
        dot(
            jnp.concatenate([pick_high, pick_high], axis=1),
            jnp.concatenate([lap_high, lap_low], axis=0),
        )
        + dot(pick_low, lap_high)
    )
    op_twice = jnp.concatenate([op_high, op_high], axis=1)

    def first_rows(op):
        return jnp.concatenate([op[COLS:], op[:NY], op[COLS - NY : COLS]], axis=0)

    border_twice, border_low = first_rows(op_twice), first_rows(op_low)

    def weigh(r, field, copies):
        high, low = split(field)
        both = jnp.concatenate([high, low], axis=0)
        border = dot(border_twice, both) + dot(border_low, high)
        for i in range(8):
            edges[r, i] = border[i : i + 1]
        tsum[r, pl.ds(0, NY)] = border[8 : 8 + NY]
        tsum[r, pl.ds(COLS - NY, NY)] = border[8 + NY :]
        if r == 0:
            ready(1, 11)
        for copy in copies[4:] + copies[2:4] + copies[:2]:
            copy.start()
        middle = slice(NY, COLS - NY)
        tsum[r, pl.ds(NY, COLS - 2 * NY)] = dot(op_twice[middle], both) + dot(op_low[middle], high)

    kind = [0, 0, 1, 1, 2, 2, 2, 2]

    def halo(r):
        plan = [
            (tsum.at[r, pl.ds(0, NY)], xin.at[r, 1]),
            (tsum.at[r, pl.ds(COLS - NY, NY)], xin.at[r, 0]),
            (edges.at[r, pl.ds(0, 4)], yin.at[r, 1]),
            (edges.at[r, pl.ds(4, 4)], yin.at[r, 0]),
            (edges.at[r, 0], cin.at[r, 3]),
            (edges.at[r, 4], cin.at[r, 2]),
            (edges.at[r, 3], cin.at[r, 1]),
            (edges.at[r, 7], cin.at[r, 0]),
        ]
        copies = [
            pltpu.make_async_remote_copy(
                src_ref=src, dst_ref=dst, send_sem=hs_sem.at[r, kind[i]], recv_sem=hr_sem.at[r, kind[i]],
                device_id=around[i], device_id_type=MESH,
            )
            for i, (src, dst) in enumerate(plan)
        ]
        whole = [
            pltpu.make_async_remote_copy(
                src_ref=box.at[r], dst_ref=box.at[r],
                send_sem=hs_sem.at[r, i], recv_sem=hr_sem.at[r, i],
                device_id=(right, my), device_id_type=MESH,
            )
            for i, box in enumerate((xin, yin, cin))
        ]
        return copies, whole

    def assemble(r):
        acc[pl.ds(0, NY), :] = tsum[r, pl.ds(0, NY)] + xin[r, 0]
        acc[pl.ds(NY, COLS - 2 * NY), :] = tsum[r, pl.ds(NY, COLS - 2 * NY)]
        acc[pl.ds(COLS - NY, NY), :] = tsum[r, pl.ds(COLS - NY, NY)] + xin[r, 1]
        corner = {0: (0, 1), 3: (2, 3)}
        for x in range(NX):
            low, high = yin[r, 0, x], yin[r, 1, x]
            if x in corner:
                low = low + cin[r, corner[x][0]]
                high = high + cin[r, corner[x][1]]
            acc[pl.ds(NY * x, 1), :] = acc[pl.ds(NY * x, 1), :] + low
            acc[pl.ds(NY * x + NY - 1, 1), :] = acc[pl.ds(NY * x + NY - 1, 1), :] + high
        return inv_col * acc[...]

    (first, first_all), (second, second_all) = halo(0), halo(1)

    def exchange(which, box, source):
        copies = [
            pltpu.make_async_remote_copy(
                src_ref=source(q), dst_ref=box.at[me],
                send_sem=gs_sem.at[which], recv_sem=gr_sem.at[which],
                device_id=(q, my), device_id_type=MESH,
            )
            for q in peers
        ]
        every = pltpu.make_async_remote_copy(
            src_ref=box.at[pl.ds(0, n_gx - 1)], dst_ref=box.at[pl.ds(0, n_gx - 1)],
            send_sem=gs_sem.at[which], recv_sem=gr_sem.at[which],
            device_id=(right, my), device_id_type=MESH,
        )
        return copies, every

    slot_sends, slot_all = exchange(0, sl, lambda q: sl.at[me])
    coef_sends, coef_all = exchange(1, got, lambda q: sent.at[q])

    def pivots():
        for load in loads[:1] + loads[7:9]:
            load.wait()
        diff = coef[pl.ds(0, LEV), :]
        above = jnp.where(level == 0, 0.0, diff)
        below = jnp.where(level == LEV - 1, 0.0, pltpu.roll(diff, LEV - 1, 0))
        surface = jnp.where(level == LEV - 1, diff[0:1], 0.0)
        centre = 1.0 + above + below + surface
        gain = jnp.zeros((1, COLS), F32)
        for k in range(LEV):
            scale = 1.0 / (centre[k : k + 1] - above[k : k + 1] * gain)
            gain = below[k : k + 1] * scale
            coef[pl.ds(LEV + k, 1), :] = scale

    def ask():
        loads[6].wait()
        ready(0, n_gx - 1)
        for copy in slot_sends:
            copy.start()

    def answer():
        spread = jnp.where(
            iota((COLS, n_gx), 0) // per == iota((COLS, n_gx), 1), 1.0, 0.0
        ).astype(BF16)
        table = coef[...]
        late = table[COLS:].T
        main = table[:COLS].T
        blank = jnp.zeros((COLS, 4 * LEV - COLS), F32)
        rest = jnp.concatenate(
            [jnp.concatenate([late, blank], axis=1), jnp.concatenate([blank, late], axis=1)],
            axis=0,
        )
        slot_all.wait_recv()
        every = jnp.concatenate([sl[:, x, :] for x in range(NX)], axis=1)
        mine = (every // COLS) == me
        before = dot(jnp.where(mine, 1.0, 0.0).astype(BF16), tri)
        ranked = jnp.where(mine, before, -1.0).astype(BF16)
        within = (every % COLS).astype(F32).astype(BF16)
        hit = dot(spread, ranked) == (rows % per).astype(F32)
        chosen = jnp.sum(jnp.where(hit, dot(spread, within), 0.0), axis=1, keepdims=True)
        onehot = jnp.where(chosen == lanes.astype(F32), 1.0, 0.0)
        sent[:, pl.ds(0, per), :] = exact(onehot, main, ((1,), (0,))).reshape(n_gx, per, COLS)
        halves = onehot.reshape(n_gx, 2, half, COLS)
        halves = jnp.concatenate(
            [halves[:, i].reshape(COLS // 2, COLS) for i in range(2)], axis=1
        )
        sent[:, pl.ds(per, half), :] = exact(halves, rest, ((1,), (0,))).reshape(n_gx, half, COLS)
        for copy in coef_sends:
            copy.start()
        got[me] = sent[me]

    def pass_edges():
        loads[5].wait()
        weigh(0, v[...].reshape(COLS, FLD), first)

    def pass_again():
        for copy in first_all:
            copy.wait_recv()
        weigh(1, assemble(0), second)

    early = lax.rem(my, Z) < 2

    @pl.when(early)
    def _():
        pivots()
        ask()

    pass_edges()

    @pl.when(early)
    def _():
        answer()

    @pl.when(jnp.logical_not(early))
    def _():
        pivots()
        ask()

    pass_again()

    @pl.when(jnp.logical_not(early))
    def _():
        answer()

    own = as_row(sl[me])
    span = own // COLS
    member = jnp.where(span == iota((n_gx, COLS), 0), 1.0, 0.0)
    before = dot(member.astype(BF16), tri)
    rank = jnp.sum(member * before, axis=0, keepdims=True)
    place = span * per + rank.astype(jnp.int32)
    order = jnp.where(rows == place, 1.0, 0.0)
    pair = iota((COLS // 2, COLS), 0)
    pair = (pair // half) * per + pair % half
    order_two = jnp.concatenate(
        [jnp.where(pair == place, 1.0, 0.0), jnp.where(pair + half == place, 1.0, 0.0)], axis=0
    )

    coef_all.wait_recv()
    box = got[:, pl.ds(0, per), :].reshape(COLS, COLS)
    tail = got[:, pl.ds(per, half), :].reshape(COLS // 2, COLS)
    wide = COLS // 2
    tail = jnp.concatenate([tail[:, :wide], tail[:, wide:]], axis=0)
    early = exact(box, order, ((0,), (0,)))
    late = exact(tail, order_two, ((0,), (0,)))
    diff, scale = early[:LEV], early[LEV : 2 * LEV]
    fall = jnp.concatenate([early[2 * LEV :], late[: 3 * LEV - COLS]], axis=0)
    cloud = late[3 * LEV - COLS :]
    fac[0] = jnp.where(level == 0, 0.0, diff) * scale
    fac[1] = jnp.where(level == LEV - 1, 0.0, pltpu.roll(diff, LEV - 1, 0)) * scale
    fac[2] = scale
    settle = 1.0 / (1.0 + fall)
    fac[3] = settle
    fac[4] = jnp.where(level == 0, 0.0, pltpu.roll(fall, 1, 0)) * settle
    fac[5] = cloud * 0.5
    for source, target, steps in (
        (0, 6, range(RUN)), (1, 7, reversed(range(RUN))), (4, 8, range(RUN))
    ):
        product = None
        for i in steps:
            at = pl.ds(i, RUNS, stride=RUN)
            term = fac[source, at, :]
            product = term if product is None else product * term
            fac[target, at, :] = product

    loads[9].wait()
    for copy in second_all:
        copy.wait_recv()
    dyn[:, pl.ds(0, FLD)] = v[...].reshape(COLS, FLD) - hyp[...] * assemble(1)
    for j in range(5):
        tr[pl.ds(COLS * j, COLS), :] = dyn[:, pl.ds(COLS * j, COLS)].T
    slot_all.wait_send()
    coef_all.wait_send()
    for copy in first_all + second_all:
        copy.wait_send()


def columns(tin, fac, out, tr, wk, rain, res, sem):
    def strided(k):
        return pl.ds(k, VARS, stride=LEV)

    def row(which, k):
        return fac[which, pl.ds(k, 1), :]

    value = [None] * RUNS
    for i in range(RUN):
        for r in range(RUNS):
            k = RUN * r + i
            term = tin[strided(k), :] * row(2, k)
            value[r] = term if i == 0 else term + row(0, k) * value[r]
            wk[k] = value[r]
    for r in range(1, RUNS):
        value[r] = value[r] + row(6, RUN * r + RUN - 1) * value[r - 1]
    ends, value = value, [None] * RUNS
    for i in reversed(range(RUN)):
        for r in range(RUNS):
            k = RUN * r + i
            term = wk[k] if r == 0 else wk[k] + row(6, k) * ends[r - 1]
            value[r] = term if i == RUN - 1 else term + row(1, k) * value[r]
            wk[k] = value[r]
    for r in reversed(range(RUNS - 1)):
        value[r] = value[r] + row(7, RUN * r) * value[r + 1]
    for k in range(LEV):
        r = k // RUN
        tr[strided(k), :] = wk[k] if r == RUNS - 1 else wk[k] + row(7, k) * value[r + 1]

    def emit(j):
        width = min(COLS, FLD - COLS * j)
        part = tr[pl.ds(COLS * j, COLS), :].T[:, :width].reshape(NX, NY, width)
        res[:, :, pl.ds(COLS * j, width)] = part

    for j in (2, 3, 4):
        emit(j)
    high = pl.ds(2 * COLS, FLD - 2 * COLS)
    stores = [pltpu.make_async_copy(res.at[:, :, high], out.at[:, :, high], sem.at[0])]
    stores[0].start()

    heat, vapour, liquid = (tr[pl.ds(LEV * j, LEV), :] for j in range(3))
    moved = fac[5] * jnp.maximum(vapour - 0.3 * heat, 0.0)
    tr[pl.ds(0, LEV), :] = heat + 2.0 * moved
    tr[pl.ds(LEV, LEV), :] = vapour - moved
    rain[...] = (liquid + moved) * fac[3]
    drop = None
    for i in range(RUN):
        at = pl.ds(i, RUNS, stride=RUN)
        drop = rain[at, :] if i == 0 else rain[at, :] + fac[4, at, :] * drop
        rain[at, :] = drop
    end = None
    for r in range(RUNS):
        part = rain[pl.ds(RUN * r, RUN), :]
        if r:
            part = part + fac[8, pl.ds(RUN * r, RUN), :] * end
        tr[pl.ds(2 * LEV + RUN * r, RUN), :] = part
        end = part[RUN - 1 :]
    for j in (0, 1):
        emit(j)
    low = pl.ds(0, 2 * COLS)
    stores.append(pltpu.make_async_copy(res.at[:, :, low], out.at[:, :, low], sem.at[1]))
    stores[1].start()
    for store in stores:
        store.wait()


def solution(mesh):
    n_gx, n_gy = mesh.shape["gx"], mesh.shape["gy"]
    per = COLS // n_gx
    lap, pick = tables()
    anywhere = pl.BlockSpec(memory_space=pl.ANY)
    inside = pl.BlockSpec(memory_space=pltpu.VMEM)
    dma = pltpu.SemaphoreType.DMA

    def local(state, hyper, pmass, imass, slots, vdiff, frate, cfrac):
        fields, factors = pl.pallas_call(
            functools.partial(body, n_gx, n_gy),
            out_shape=(pltpu.VMEM((5 * COLS, COLS), F32), pltpu.VMEM((9, LEV, COLS), F32)),
            in_specs=[anywhere] * 10,
            out_specs=(inside, inside),
            scratch_shapes=[
                pltpu.VMEM((NX, NY, FLD), F32),
                pltpu.VMEM((2, COLS, FLD), F32),
                pltpu.VMEM((COLS, FLD), F32),
                pltpu.VMEM((2, 8, 1, FLD), F32),
                pltpu.VMEM((2, 2, NY, FLD), F32),
                pltpu.VMEM((2, 2, 4, 1, FLD), F32),
                pltpu.VMEM((2, 4, 1, FLD), F32),
                pltpu.VMEM((2, NX, NY), F32),
                pltpu.VMEM((n_gx, NX, NY), jnp.int32),
                pltpu.VMEM((4 * LEV, COLS), F32),
                pltpu.VMEM((n_gx, per + per // 2, COLS), F32),
                pltpu.VMEM((n_gx, per + per // 2, COLS), F32),
                pltpu.VMEM((COLS, COLS), F32),
                pltpu.VMEM((COLS + 8, COLS), F32),
                pltpu.VMEM((1, FLD), F32),
                pltpu.VMEM((COLS, 5 * COLS), F32),
                dma((10,)),
                dma((2, 3)),
                dma((2, 3)),
                dma((2,)),
                dma((2,)),
                pltpu.SemaphoreType.REGULAR((2,)),
            ],
            compiler_params=pltpu.CompilerParams(collective_id=0, has_side_effects=True),
        )(state, hyper, pmass, imass, slots, vdiff, frate, cfrac,
          jnp.asarray(lap), jnp.asarray(pick))
        return pl.pallas_call(
            columns,
            out_shape=jax.ShapeDtypeStruct((NX, NY, FLD), F32),
            in_specs=[inside, inside],
            out_specs=anywhere,
            scratch_shapes=[
                pltpu.VMEM((5 * COLS, COLS), F32),
                pltpu.VMEM((LEV, VARS, COLS), F32),
                pltpu.VMEM((LEV, COLS), F32),
                pltpu.VMEM((NX, NY, FLD), F32),
                dma((2,)),
            ],
        )(*(pltpu.with_memory_space_constraint(x, pltpu.VMEM) for x in (fields, factors)))

    placed = (
        P("gx", "gy", None), P(), P("gx", "gy"), P("gx", "gy"), P("gx", "gy"),
        P("gy", None, "gx"), P("gy", None, "gx"), P("gy", None, "gx"),
    )
    return jax.shard_map(
        local, mesh=mesh, in_specs=placed, out_specs=P("gx", "gy", None), check_vma=False
    )
```

```python
import functools

import jax
import jax.numpy as jnp
import numpy as np
from jax import lax
from jax.experimental import pallas as pl
from jax.experimental.pallas import tpu as pltpu
from jax.sharding import PartitionSpec as P

MESH = pl.DeviceIdType.MESH
F32 = jnp.float32
BF16 = jnp.bfloat16
NX, NY, COLS, LEV, VARS = 4, 32, 128, 48, 11
Z = 8
RUN = 8
RUNS = LEV // RUN
FLD = LEV * VARS


def second_table():
    nodes = np.array([-1.0, -1.0 / np.sqrt(5.0), 1.0 / np.sqrt(5.0), 1.0])
    deriv = np.zeros((4, 4))
    for i in range(4):
        for j in range(4):
            if i == j:
                deriv[i, j] = sum(1.0 / (nodes[i] - nodes[o]) for o in range(4) if o != i)
            else:
                upper = np.prod([nodes[i] - nodes[o] for o in range(4) if o != i])
                lower = np.prod([nodes[j] - nodes[o] for o in range(4) if o != j])
                deriv[i, j] = upper / (lower * (nodes[i] - nodes[j]))
    return (deriv @ deriv).astype(np.float32)


def tables():
    second = second_table()
    x, y = np.divmod(np.arange(COLS), NY)
    same_x = x[:, None] == x[None, :]
    same_y = y[:, None] == y[None, :]
    same_e = (y[:, None] // 4) == (y[None, :] // 4)
    lap = np.where(same_y, second[x[:, None], x[None, :]], 0.0)
    lap = lap + np.where(same_x & same_e, second[y[:, None] % 4, y[None, :] % 4], 0.0)
    twin = np.where(y % 4 == 0, y - 1, np.where(y % 4 == 3, y + 1, -5))
    pick = np.eye(COLS) + np.where(same_x & (y[None, :] == twin[:, None]), 1.0, 0.0)
    edge = np.zeros((8, COLS))
    for i in range(4):
        edge[i, i * NY] = 1.0
        edge[4 + i, i * NY + NY - 1] = 1.0
    return lap.astype(np.float32), np.concatenate([pick, edge], 0).astype(np.float32)


def split(value):
    high = value.astype(BF16)
    return high, (value - high.astype(F32)).astype(BF16)


def dot(a, b):
    return jnp.dot(a, b, preferred_element_type=F32)


def exact(a, b, dims):
    return lax.dot_general(
        a, b, (dims, ((), ())), precision=lax.Precision.HIGHEST, preferred_element_type=F32
    )


def iota(shape, dim):
    return lax.broadcasted_iota(jnp.int32, shape, dim)


def body(
    n_gx, n_gy,
    state, hyper, pmass, imass, slots, vdiff, frate, cfrac, lap, pick,
    tr, fac,
    v, tsum, acc, edges, xin, yin, cin, small, sl, coef, sent, got, lap_s, pick_s, hyp, dyn,
    in_sem, hs_sem, hr_sem, gs_sem, gr_sem, here_sem,
):
    per = COLS // n_gx
    half = per // 2
    me = lax.axis_index("gx")
    my = lax.axis_index("gy")
    left, right = lax.rem(me + n_gx - 1, n_gx), lax.rem(me + 1, n_gx)
    down, up = lax.rem(my + n_gy - 1, n_gy), lax.rem(my + 1, n_gy)
    far_first = sorted(range(1, n_gx), key=lambda i: -min(i, n_gx - i))
    peers = [lax.rem(me + i, n_gx) for i in far_first]
    core = lax.rem(me, 2)
    chip = me // 2
    beside = lax.rem(chip + n_gx // 2 - 1 + 2 * core, n_gx // 2)
    around = [(left, my), (right, my), (me, down), (me, up),
              (left, down), (left, up), (right, down), (right, up)]

    loads = [
        pltpu.make_async_copy(vdiff.at[0], coef.at[pl.ds(0, LEV)], in_sem.at[0]),
        pltpu.make_async_copy(pmass, small.at[0], in_sem.at[1]),
        pltpu.make_async_copy(imass, small.at[1], in_sem.at[2]),
        pltpu.make_async_copy(lap, lap_s, in_sem.at[3]),
        pltpu.make_async_copy(pick, pick_s, in_sem.at[4]),
        pltpu.make_async_copy(state, v, in_sem.at[5]),
        pltpu.make_async_copy(slots, sl.at[me], in_sem.at[6]),
        pltpu.make_async_copy(frate.at[0], coef.at[pl.ds(2 * LEV, LEV)], in_sem.at[7]),
        pltpu.make_async_copy(cfrac.at[0], coef.at[pl.ds(3 * LEV, LEV)], in_sem.at[8]),
        pltpu.make_async_copy(hyper, hyp.at[0], in_sem.at[9]),
    ]
    for load in loads[5:6] + loads[1:5]:
        load.start()
    barrier = pltpu.get_barrier_semaphore()

    def arrive(gx, gy):
        pl.semaphore_signal(barrier, inc=1, device_id=(gx, gy), device_id_type=MESH)

    for gy in (down, up):
        arrive(2 * beside + 1, gy)
        arrive(2 * chip + 1, gy)
    arrive(2 * beside + 1, my)
    for i in sorted(range(1, n_gx // 2), key=lambda i: -min(i, n_gx // 2 - i)):
        arrive(2 * lax.rem(chip + i, n_gx // 2), my)

    @pl.when(core == 0)
    def _():
        arrive(me + 1, my)

    @pl.when(core == 1)
    def _():
        arrive(me - 1, my)

    def ready(counter, amount):
        partner = me + 1 - 2 * core

        @pl.when(core == counter)
        def _():
            pl.semaphore_wait(barrier, amount)
            pl.semaphore_signal(
                here_sem.at[counter], inc=1, device_id=(partner, my), device_id_type=MESH
            )

        @pl.when(core != counter)
        def _():
            pl.semaphore_wait(here_sem.at[counter], 1)

    for load in loads[:1] + loads[6:]:
        load.start()

    rows, lanes = iota((COLS, COLS), 0), iota((COLS, COLS), 1)
    tri = jnp.where(rows < lanes, 1.0, 0.0).astype(BF16)
    level = iota((LEV, COLS), 0)

    def as_row(block):
        return jnp.concatenate([block[x : x + 1, :] for x in range(NX)], axis=1)

    for load in loads[1:5]:
        load.wait()
    mass_row = as_row(small[0])
    inv_row = as_row(small[1])
    inv_col = jnp.sum(jnp.where(rows == lanes, inv_row, 0.0), axis=1, keepdims=True)
    pick_high, pick_low = split(pick_s[...] * mass_row)
    lap_high, lap_low = split(lap_s[...])
    op_high, op_low = split(
        dot(
            jnp.concatenate([pick_high, pick_high], axis=1),
            jnp.concatenate([lap_high, lap_low], axis=0),
        )
        + dot(pick_low, lap_high)
    )
    op_twice = jnp.concatenate([op_high, op_high], axis=1)

    def first_rows(op):
        return jnp.concatenate([op[COLS:], op[:NY], op[COLS - NY : COLS]], axis=0)

    border_twice, border_low = first_rows(op_twice), first_rows(op_low)

    def weigh(r, field, copies):
        high, low = split(field)
        both = jnp.concatenate([high, low], axis=0)
        border = dot(border_twice, both) + dot(border_low, high)
        for i in range(8):
            edges[r, i] = border[i : i + 1]
        tsum[r, pl.ds(0, NY)] = border[8 : 8 + NY]
        tsum[r, pl.ds(COLS - NY, NY)] = border[8 + NY :]
        if r == 0:
            ready(1, 11)
        for copy in copies[4:] + copies[2:4] + copies[:2]:
            copy.start()
        middle = slice(NY, COLS - NY)
        tsum[r, pl.ds(NY, COLS - 2 * NY)] = dot(op_twice[middle], both) + dot(op_low[middle], high)

    kind = [0, 0, 1, 1, 2, 2, 2, 2]

    def halo(r):
        plan = [
            (tsum.at[r, pl.ds(0, NY)], xin.at[r, 1]),
            (tsum.at[r, pl.ds(COLS - NY, NY)], xin.at[r, 0]),
            (edges.at[r, pl.ds(0, 4)], yin.at[r, 1]),
            (edges.at[r, pl.ds(4, 4)], yin.at[r, 0]),
            (edges.at[r, 0], cin.at[r, 3]),
            (edges.at[r, 4], cin.at[r, 2]),
            (edges.at[r, 3], cin.at[r, 1]),
            (edges.at[r, 7], cin.at[r, 0]),
        ]
        copies = [
            pltpu.make_async_remote_copy(
                src_ref=src, dst_ref=dst, send_sem=hs_sem.at[r, kind[i]], recv_sem=hr_sem.at[r, kind[i]],
                device_id=around[i], device_id_type=MESH,
            )
            for i, (src, dst) in enumerate(plan)
        ]
        whole = [
            pltpu.make_async_remote_copy(
                src_ref=box.at[r], dst_ref=box.at[r],
                send_sem=hs_sem.at[r, i], recv_sem=hr_sem.at[r, i],
                device_id=(right, my), device_id_type=MESH,
            )
            for i, box in enumerate((xin, yin, cin))
        ]
        return copies, whole

    def own_part(r):
        acc[...] = inv_col * tsum[r]

    def assemble(r, whole):
        whole[0].wait_recv()
        for part, at in ((0, 0), (1, COLS - NY)):
            scale = inv_col[at : at + NY]
            acc[pl.ds(at, NY), :] = acc[pl.ds(at, NY), :] + scale * xin[r, part]
        whole[1].wait_recv()
        whole[2].wait_recv()
        corner = {0: (0, 1), 3: (2, 3)}
        for x in range(NX):
            low, high = yin[r, 0, x], yin[r, 1, x]
            if x in corner:
                low = low + cin[r, corner[x][0]]
                high = high + cin[r, corner[x][1]]
            for at, value in ((NY * x, low), (NY * x + NY - 1, high)):
                acc[pl.ds(at, 1), :] = acc[pl.ds(at, 1), :] + inv_col[at : at + 1] * value
        return acc[...]

    (first, first_all), (second, second_all) = halo(0), halo(1)

    def exchange(which, box, source):
        copies = [
            pltpu.make_async_remote_copy(
                src_ref=source(q), dst_ref=box.at[me],
                send_sem=gs_sem.at[which], recv_sem=gr_sem.at[which],
                device_id=(q, my), device_id_type=MESH,
            )
            for q in peers
        ]
        every = pltpu.make_async_remote_copy(
            src_ref=box.at[pl.ds(0, n_gx - 1)], dst_ref=box.at[pl.ds(0, n_gx - 1)],
            send_sem=gs_sem.at[which], recv_sem=gr_sem.at[which],
            device_id=(right, my), device_id_type=MESH,
        )
        return copies, every

    slot_sends, slot_all = exchange(0, sl, lambda q: sl.at[me])
    coef_sends, coef_all = exchange(1, got, lambda q: sent.at[q])

    def pivots():
        for load in loads[:1] + loads[7:9]:
            load.wait()
        diff = coef[pl.ds(0, LEV), :]
        above = jnp.where(level == 0, 0.0, diff)
        below = jnp.where(level == LEV - 1, 0.0, pltpu.roll(diff, LEV - 1, 0))
        surface = jnp.where(level == LEV - 1, diff[0:1], 0.0)
        centre = 1.0 + above + below + surface
        gain = jnp.zeros((1, COLS), F32)
        for k in range(LEV):
            scale = 1.0 / (centre[k : k + 1] - above[k : k + 1] * gain)
            gain = below[k : k + 1] * scale
            coef[pl.ds(LEV + k, 1), :] = scale

    def ask():
        loads[6].wait()
        ready(0, n_gx - 1)
        for copy in slot_sends:
            copy.start()

    def answer():
        spread = jnp.where(
            iota((COLS, n_gx), 0) // per == iota((COLS, n_gx), 1), 1.0, 0.0
        ).astype(BF16)
        table = coef[...]
        late = table[COLS:].T
        main = table[:COLS].T
        blank = jnp.zeros((COLS, 4 * LEV - COLS), F32)
        rest = jnp.concatenate(
            [jnp.concatenate([late, blank], axis=1), jnp.concatenate([blank, late], axis=1)],
            axis=0,
        )
        slot_all.wait_recv()
        every = jnp.concatenate([sl[:, x, :] for x in range(NX)], axis=1)
        mine = (every // COLS) == me
        before = dot(jnp.where(mine, 1.0, 0.0).astype(BF16), tri)
        ranked = jnp.where(mine, before, -1.0).astype(BF16)
        within = (every % COLS).astype(F32).astype(BF16)
        hit = dot(spread, ranked) == (rows % per).astype(F32)
        chosen = jnp.sum(jnp.where(hit, dot(spread, within), 0.0), axis=1, keepdims=True)
        onehot = jnp.where(chosen == lanes.astype(F32), 1.0, 0.0)
        sent[:, pl.ds(0, per), :] = exact(onehot, main, ((1,), (0,))).reshape(n_gx, per, COLS)
        halves = onehot.reshape(n_gx, 2, half, COLS)
        halves = jnp.concatenate(
            [halves[:, i].reshape(COLS // 2, COLS) for i in range(2)], axis=1
        )
        sent[:, pl.ds(per, half), :] = exact(halves, rest, ((1,), (0,))).reshape(n_gx, half, COLS)
        for copy in coef_sends:
            copy.start()
        got[me] = sent[me]

    def pass_edges():
        loads[5].wait()
        weigh(0, v[...].reshape(COLS, FLD), first)

    def pass_again():
        own_part(0)
        weigh(1, assemble(0, first_all), second)
        own_part(1)

    early = lax.rem(my, Z) < 2

    @pl.when(early)
    def _():
        pivots()
        ask()

    pass_edges()

    @pl.when(early)
    def _():
        answer()

    @pl.when(jnp.logical_not(early))
    def _():
        pivots()
        ask()

    pass_again()

    @pl.when(jnp.logical_not(early))
    def _():
        answer()

    own = as_row(sl[me])
    span = own // COLS
    member = jnp.where(span == iota((n_gx, COLS), 0), 1.0, 0.0)
    before = dot(member.astype(BF16), tri)
    rank = jnp.sum(member * before, axis=0, keepdims=True)
    place = span * per + rank.astype(jnp.int32)
    order = jnp.where(rows == place, 1.0, 0.0)
    pair = iota((COLS // 2, COLS), 0)
    pair = (pair // half) * per + pair % half
    order_two = jnp.concatenate(
        [jnp.where(pair == place, 1.0, 0.0), jnp.where(pair + half == place, 1.0, 0.0)], axis=0
    )

    coef_all.wait_recv()
    box = got[:, pl.ds(0, per), :].reshape(COLS, COLS)
    tail = got[:, pl.ds(per, half), :].reshape(COLS // 2, COLS)
    wide = COLS // 2
    tail = jnp.concatenate([tail[:, :wide], tail[:, wide:]], axis=0)
    early = exact(box, order, ((0,), (0,)))
    late = exact(tail, order_two, ((0,), (0,)))
    diff, scale = early[:LEV], early[LEV : 2 * LEV]
    fall = jnp.concatenate([early[2 * LEV :], late[: 3 * LEV - COLS]], axis=0)
    cloud = late[3 * LEV - COLS :]
    fac[0] = jnp.where(level == 0, 0.0, diff) * scale
    fac[1] = jnp.where(level == LEV - 1, 0.0, pltpu.roll(diff, LEV - 1, 0)) * scale
    fac[2] = scale
    settle = 1.0 / (1.0 + fall)
    fac[3] = settle
    fac[4] = jnp.where(level == 0, 0.0, pltpu.roll(fall, 1, 0)) * settle
    fac[5] = cloud * 0.5
    for source, target, steps in (
        (0, 6, range(RUN)), (1, 7, reversed(range(RUN))), (4, 8, range(RUN))
    ):
        product = None
        for i in steps:
            at = pl.ds(i, RUNS, stride=RUN)
            term = fac[source, at, :]
            product = term if product is None else product * term
            fac[target, at, :] = product

    loads[9].wait()
    dyn[:, pl.ds(0, FLD)] = v[...].reshape(COLS, FLD) - hyp[...] * assemble(1, second_all)
    for j in range(5):
        tr[pl.ds(COLS * j, COLS), :] = dyn[:, pl.ds(COLS * j, COLS)].T
    slot_all.wait_send()
    coef_all.wait_send()
    for copy in first_all + second_all:
        copy.wait_send()


def columns(tin, fac, out, tr, wk, rain, res, sem):
    def strided(k):
        return pl.ds(k, VARS, stride=LEV)

    def row(which, k):
        return fac[which, pl.ds(k, 1), :]

    value = [None] * RUNS
    for i in range(RUN):
        for r in range(RUNS):
            k = RUN * r + i
            term = tin[strided(k), :] * row(2, k)
            value[r] = term if i == 0 else term + row(0, k) * value[r]
            wk[k] = value[r]
    for r in range(1, RUNS):
        value[r] = value[r] + row(6, RUN * r + RUN - 1) * value[r - 1]
    ends, value = value, [None] * RUNS
    for i in reversed(range(RUN)):
        for r in range(RUNS):
            k = RUN * r + i
            term = wk[k] if r == 0 else wk[k] + row(6, k) * ends[r - 1]
            value[r] = term if i == RUN - 1 else term + row(1, k) * value[r]
            wk[k] = value[r]
    for r in reversed(range(RUNS - 1)):
        value[r] = value[r] + row(7, RUN * r) * value[r + 1]
    for k in range(LEV):
        r = k // RUN
        tr[strided(k), :] = wk[k] if r == RUNS - 1 else wk[k] + row(7, k) * value[r + 1]

    def emit(j):
        width = min(COLS, FLD - COLS * j)
        part = tr[pl.ds(COLS * j, COLS), :].T[:, :width].reshape(NX, NY, width)
        res[:, :, pl.ds(COLS * j, width)] = part

    for j in (2, 3, 4):
        emit(j)
    high = pl.ds(2 * COLS, FLD - 2 * COLS)
    stores = [pltpu.make_async_copy(res.at[:, :, high], out.at[:, :, high], sem.at[0])]
    stores[0].start()

    heat, vapour, liquid = (tr[pl.ds(LEV * j, LEV), :] for j in range(3))
    moved = fac[5] * jnp.maximum(vapour - 0.3 * heat, 0.0)
    tr[pl.ds(0, LEV), :] = heat + 2.0 * moved
    tr[pl.ds(LEV, LEV), :] = vapour - moved
    rain[...] = (liquid + moved) * fac[3]
    drop = None
    for i in range(RUN):
        at = pl.ds(i, RUNS, stride=RUN)
        drop = rain[at, :] if i == 0 else rain[at, :] + fac[4, at, :] * drop
        rain[at, :] = drop
    end = None
    for r in range(RUNS):
        part = rain[pl.ds(RUN * r, RUN), :]
        if r:
            part = part + fac[8, pl.ds(RUN * r, RUN), :] * end
        tr[pl.ds(2 * LEV + RUN * r, RUN), :] = part
        end = part[RUN - 1 :]
    for j in (0, 1):
        emit(j)
    low = pl.ds(0, 2 * COLS)
    stores.append(pltpu.make_async_copy(res.at[:, :, low], out.at[:, :, low], sem.at[1]))
    stores[1].start()
    for store in stores:
        store.wait()


def solution(mesh):
    n_gx, n_gy = mesh.shape["gx"], mesh.shape["gy"]
    per = COLS // n_gx
    lap, pick = tables()
    anywhere = pl.BlockSpec(memory_space=pl.ANY)
    inside = pl.BlockSpec(memory_space=pltpu.VMEM)
    dma = pltpu.SemaphoreType.DMA

    def local(state, hyper, pmass, imass, slots, vdiff, frate, cfrac):
        fields, factors = pl.pallas_call(
            functools.partial(body, n_gx, n_gy),
            out_shape=(pltpu.VMEM((5 * COLS, COLS), F32), pltpu.VMEM((9, LEV, COLS), F32)),
            in_specs=[anywhere] * 10,
            out_specs=(inside, inside),
            scratch_shapes=[
                pltpu.VMEM((NX, NY, FLD), F32),
                pltpu.VMEM((2, COLS, FLD), F32),
                pltpu.VMEM((COLS, FLD), F32),
                pltpu.VMEM((2, 8, 1, FLD), F32),
                pltpu.VMEM((2, 2, NY, FLD), F32),
                pltpu.VMEM((2, 2, 4, 1, FLD), F32),
                pltpu.VMEM((2, 4, 1, FLD), F32),
                pltpu.VMEM((2, NX, NY), F32),
                pltpu.VMEM((n_gx, NX, NY), jnp.int32),
                pltpu.VMEM((4 * LEV, COLS), F32),
                pltpu.VMEM((n_gx, per + per // 2, COLS), F32),
                pltpu.VMEM((n_gx, per + per // 2, COLS), F32),
                pltpu.VMEM((COLS, COLS), F32),
                pltpu.VMEM((COLS + 8, COLS), F32),
                pltpu.VMEM((1, FLD), F32),
                pltpu.VMEM((COLS, 5 * COLS), F32),
                dma((10,)),
                dma((2, 3)),
                dma((2, 3)),
                dma((2,)),
                dma((2,)),
                pltpu.SemaphoreType.REGULAR((2,)),
            ],
            compiler_params=pltpu.CompilerParams(collective_id=0, has_side_effects=True),
        )(state, hyper, pmass, imass, slots, vdiff, frate, cfrac,
          jnp.asarray(lap), jnp.asarray(pick))
        return pl.pallas_call(
            columns,
            out_shape=jax.ShapeDtypeStruct((NX, NY, FLD), F32),
            in_specs=[inside, inside],
            out_specs=anywhere,
            scratch_shapes=[
                pltpu.VMEM((5 * COLS, COLS), F32),
                pltpu.VMEM((LEV, VARS, COLS), F32),
                pltpu.VMEM((LEV, COLS), F32),
                pltpu.VMEM((NX, NY, FLD), F32),
                dma((2,)),
            ],
        )(*(pltpu.with_memory_space_constraint(x, pltpu.VMEM) for x in (fields, factors)))

    placed = (
        P("gx", "gy", None), P(), P("gx", "gy"), P("gx", "gy"), P("gx", "gy"),
        P("gy", None, "gx"), P("gy", None, "gx"), P("gy", None, "gx"),
    )
    return jax.shard_map(
        local, mesh=mesh, in_specs=placed, out_specs=P("gx", "gy", None), check_vma=False
    )
```
